32 devices in a mesh: pts: 8 (over z, y), feat: 4 (over x, core).
Axes of the slice: x: 2, y: 2, z: 4, core: 2. Of those that a mesh axis runs over, the one named last changes fastest.
Arguments:
- slab: bfloat16 [16384, 768], P('pts', 'feat'), may hold values from -40 to 40
- centres: bfloat16 [4096, 768], replicated, may hold values from -3 to 3
- labels: int32 [16384, 1], P(('pts', 'feat')), may hold values from 0 to 4095
- sample_rows: int32 [8, 8, 4], P('pts'), may hold values from 0 to 2047, as said below
- sample_count: int32 [8, 8], P('pts'), may hold values from 0 to 4, as said below
- slot_offset: int32 [8, 8], P('pts'), may hold values from 0 to 28, as said below
Outputs:
- coreset: bfloat16 [256, 768], P('pts', 'feat')
The draws below stay inside these ranges and needn't reach their ends.
Inputs may be any that keep to these rules, and one draw needn't show every extreme that they name: `sample_rows`: row indices within a source shard; sampled independently with replacement. `sample_count`: in every draw some owner receives 4 rows from every source. slot_offset[o,p] is the sum of sample_count[q,o] over sources q < p.
All inputs are finite; a program needn't handle non-finite values.
Results may differ from the reference program's by a relative error of at most 0.0006.
Values may be sent and summed in bfloat16 or wider, within the bound.
A program may use at most 64 MiB of HBM per device.

```python
import math
import jax
import jax.numpy as jnp
from jax import lax

D = 768
CENTRES = 4096
CAP = 4
ROWS_PTS = 2048
NPTS = 16384
SOURCES = 8
OWNERS = 8
OWN_CAP = 32


def draw_slab(key, part):
    key_base, key_row, key_col = jax.random.split(key, 3)
    row_scale = jnp.exp(jax.random.uniform(key_row, (NPTS, 1), jnp.float32, math.log(0.3), math.log(3.0)))
    col_scale = jnp.exp(jax.random.uniform(key_col, (1, D), jnp.float32, math.log(0.3), math.log(3.0))) / 1.4
    base_vals = jax.random.normal(key_base, (NPTS, D), jnp.float32)
    return jnp.clip(base_vals * row_scale * col_scale, -40.0, 40.0).astype(jnp.bfloat16)


def plan_full(key):
    return jax.random.randint(jax.random.fold_in(key, 7), (), 0, OWNERS, jnp.int32)


def plan_counts(key):
    base_key = jax.random.fold_in(key, 11)
    key_heavy, key_light, key_busy = jax.random.split(base_key, 3)
    heavy = jax.random.randint(key_heavy, (OWNERS,), 0, 4, jnp.int32) == 0
    light_counts = jax.random.randint(key_light, (SOURCES, OWNERS), 0, CAP, jnp.int32)
    busy_counts = jax.random.randint(key_busy, (SOURCES, OWNERS), 2, CAP + 1, jnp.int32)
    counts_all = jnp.where(heavy[None, :], busy_counts, light_counts)
    full_owner = plan_full(key)
    owner_ids = jnp.arange(OWNERS, dtype=jnp.int32)[None, :]
    return jnp.where(owner_ids == full_owner, jnp.int32(CAP), counts_all).astype(jnp.int32)


def draw_sample_count(key, part):
    return plan_counts(key)


def draw_slot_offset(key, part):
    per_owner = plan_counts(key).T
    return (jnp.cumsum(per_owner, axis=1) - per_owner).astype(jnp.int32)


def draw_sample_rows(key, part):
    row_key = jax.random.fold_in(key, 23)
    picked = jax.random.randint(row_key, (SOURCES, OWNERS, CAP), 0, ROWS_PTS, jnp.int32)
    full_owner = plan_full(key)
    owner_ids = jnp.arange(OWNERS, dtype=jnp.int32)[None, :, None]
    slot_ids = jnp.arange(CAP, dtype=jnp.int32)[None, None, :]
    source_ids = jnp.arange(SOURCES, dtype=jnp.int32)[:, None, None]
    top_spot = (owner_ids == full_owner) & (slot_ids == 0) & (source_ids == 0)
    low_spot = (owner_ids == full_owner) & (slot_ids == 1) & (source_ids == 0)
    picked = jnp.where(top_spot, jnp.int32(ROWS_PTS - 1), picked)
    return jnp.where(low_spot, jnp.int32(0), picked).astype(jnp.int32)


def touch_ends(drawn, key, least, largest):
    place = [jax.random.randint(jax.random.fold_in(key, axis), (), 0, length) for axis, length in enumerate(drawn.shape)]
    main_axis = drawn.shape.index(max(drawn.shape))
    next_to = place[:main_axis] + [(place[main_axis] + 1) % drawn.shape[main_axis]] + place[main_axis + 1:]
    return drawn.at[tuple(place)].set(least).at[tuple(next_to)].set(largest)


def gaussian(rng, dims, deviation, limit, held_as=jnp.bfloat16):
    drawn = deviation * jax.random.normal(rng, dims, jnp.float32)
    return jnp.clip(drawn, min=-limit, max=limit).astype(held_as)


def setup_inputs(seed: int = 0) -> dict:
    keys = jax.random.split(jax.random.key(seed), 7)
    slab = draw_slab(jax.random.fold_in(keys[6], 71), 0)
    centres = gaussian(keys[1], (CENTRES, D), 0.5, 3.0)
    labels = touch_ends(jax.random.randint(keys[2], (NPTS, 1), 0, CENTRES), jax.random.fold_in(keys[2], 1), 0, CENTRES - 1).astype(jnp.int32)
    sample_rows = draw_sample_rows(jax.random.fold_in(keys[6], 71), 0)
    sample_count = draw_sample_count(jax.random.fold_in(keys[6], 71), 0)
    slot_offset = draw_slot_offset(jax.random.fold_in(keys[6], 71), 0)
    return {"slab": slab, "centres": centres, "labels": labels, "sample_rows": sample_rows, "sample_count": sample_count, "slot_offset": slot_offset}


def nearest_block(points, centres, centre_sq):
    cross_term = jnp.dot(points, centres.T, preferred_element_type=jnp.float32)
    point_sq = jnp.sum(jnp.square(points.astype(jnp.float32)), axis=1)
    return jnp.min(point_sq[:, None] + centre_sq[None, :] - 2.0 * cross_term, axis=1)


def reference(slab, centres, labels, sample_rows, sample_count, slot_offset):
    centre_sq = jnp.sum(jnp.square(centres.astype(jnp.float32)), axis=1)
    blocks = slab.reshape(NPTS // ROWS_PTS, ROWS_PTS, D)
    nearest = lax.map(lambda span_rows: nearest_block(span_rows, centres, centre_sq), blocks).reshape(NPTS)
    member = labels[:, 0]
    cluster_cost = jax.ops.segment_sum(nearest, member, num_segments=CENTRES)
    cluster_size = jax.ops.segment_sum(jnp.ones_like(nearest), member, num_segments=CENTRES)
    sens = nearest / cluster_cost[member] + 1.0 / cluster_size[member]
    weight = (2.0 * CENTRES / NPTS) / sens
    global_rows = jnp.arange(SOURCES, dtype=jnp.int32)[:, None, None] * ROWS_PTS + sample_rows.astype(jnp.int32)
    chosen = slab[global_rows]
    chosen_weight = weight[global_rows]
    live_slot = jnp.arange(CAP, dtype=jnp.int32)[None, None, :] < sample_count[:, :, None]
    scaled = jnp.where(live_slot[..., None], chosen.astype(jnp.float32) * chosen_weight[..., None], jnp.float32(0.0)).astype(jnp.bfloat16)
    target = (jnp.arange(OWNERS, dtype=jnp.int32)[None, :, None] * OWN_CAP
              + slot_offset.T.astype(jnp.int32)[:, :, None]
              + jnp.arange(CAP, dtype=jnp.int32)[None, None, :])
    placed = jnp.zeros((OWNERS * OWN_CAP, D), jnp.float32)
    placed = placed.at[target.reshape(-1)].add(scaled.reshape(-1, D).astype(jnp.float32), mode="drop")
    return placed.astype(jnp.bfloat16)
```

```python
import functools

import jax
import jax.numpy as jnp
from jax import lax
from jax.experimental import pallas as pl
from jax.experimental.pallas import tpu as pltpu
from jax.sharding import PartitionSpec as P

NT = (((1,), (1,)), ((), ()))
LANES = 128
SUB = 8
CHUNK = 256
TILE = 2048
MESH = pl.DeviceIdType.MESH


def local(slab, centres, labels, sample_rows, sample_count, slot_offset):
    rows_pts, feat_width = slab.shape
    feat_count = lax.axis_size("feat")
    rows_dev = rows_pts // feat_count
    centre_count = centres.shape[0]
    centre_sq = jnp.sum(jnp.square(centres.astype(jnp.float32)), axis=1)
    stacked = slab.reshape(feat_count, rows_dev, feat_width)
    points = lax.all_to_all(stacked, "feat", split_axis=0, concat_axis=2, tiled=True)[0]
    cross_term = lax.dot_general(points, centres, NT, preferred_element_type=jnp.float32)
    point_sq = jnp.sum(jnp.square(points.astype(jnp.float32)), axis=1)
    nearest = jnp.min(point_sq[:, None] + centre_sq[None, :] - 2.0 * cross_term, axis=1)[None, :][0]
    member = labels[:, 0]
    cost_part = jax.ops.segment_sum(nearest, member, num_segments=centre_count)
    size_part = jax.ops.segment_sum(jnp.ones_like(nearest), member, num_segments=centre_count)
    cluster_cost, cluster_size = lax.psum((cost_part, size_part), ("pts", "feat"))
    own_sens = nearest / jnp.take(cluster_cost, member) + 1.0 / jnp.take(cluster_size, member)
    shard_sens = lax.all_gather(own_sens, "feat", axis=0, tiled=True)
    total_points = rows_pts * lax.axis_size("pts")
    weight = 2.0 * centre_count / total_points / shard_sens
    picked_rows = sample_rows[0]
    owner_count, slot_count = picked_rows.shape
    chosen = jnp.take(slab, picked_rows.reshape(-1), axis=0).reshape(
        owner_count, slot_count, feat_width
    )
    chosen_weight = jnp.take(weight, picked_rows)
    live_slot = jnp.arange(slot_count, dtype=jnp.int32)[None, :] < sample_count[0][:, None]
    scaled = jnp.where(
        live_slot[:, :, None], chosen.astype(jnp.float32) * chosen_weight[:, :, None], 0.0
    ).astype(jnp.bfloat16)
    arrived = lax.all_to_all(scaled, "pts", split_axis=0, concat_axis=0, tiled=True)
    target = slot_offset[0][:, None] + jnp.arange(slot_count, dtype=jnp.int32)[None, :]
    own_rows = arrived.shape[0] * slot_count
    placed = jnp.zeros((own_rows, feat_width), jnp.float32)
    placed = placed.at[target.reshape(-1)].add(
        arrived.reshape(-1, feat_width).astype(jnp.float32), mode="drop"
    )
    return placed.astype(jnp.bfloat16)


def kernel(n_p, n_f, chunks, tile, slab_hbm, labels_hbm, rows_hbm, count_hbm, offset_hbm, cen_hbm,
           out_ref, cen, csq, gap_ref, slab_ref, points_ref, labels_ref, rows_ref, count_ref, offset_ref,
           lab_msg, lab_all, row_msg, row_all, red_msg, red_all, in_sem, cen_sem, a_send, a_recv,
           lab_send, lab_recv, row_send, row_recv, red_send, red_recv):
    f32, bf16 = jnp.float32, jnp.bfloat16
    width, rows_pts = slab_ref.shape
    rows_dev = rows_pts // n_f
    crow = rows_dev // chunks
    n = n_p * n_f
    centre_count = cen.shape[0]
    slots = rows_ref.shape[1]
    tiles = centre_count // tile
    my_p, my_f = lax.axis_index("pts"), lax.axis_index("feat")
    me = my_p * n_f + my_f

    def device(d):
        other = lax.rem(me + d, n)
        return other // n_f, lax.rem(other, n_f)

    barrier = pltpu.get_barrier_semaphore()
    for d in range(1, n):
        pl.semaphore_signal(barrier, inc=1, device_id=device(d), device_id_type=MESH)

    own_k = pl.ds(pl.multiple_of(my_f * width, width), width)
    own_cols = pl.ds(pl.multiple_of(my_f * rows_dev, rows_dev), rows_dev)
    in_copies = [
        pltpu.make_async_copy(rows_hbm, rows_ref, in_sem.at[0]),
        pltpu.make_async_copy(count_hbm, count_ref, in_sem.at[1]),
        pltpu.make_async_copy(offset_hbm, offset_ref, in_sem.at[2]),
        pltpu.make_async_copy(labels_hbm, labels_ref, in_sem.at[3]),
        pltpu.make_async_copy(slab_hbm, slab_ref, in_sem.at[4]),
        pltpu.make_async_copy(slab_hbm.at[:, own_cols], points_ref.at[own_k], in_sem.at[5]),
    ]
    for copy in in_copies:
        copy.start()
    cen_copies = []
    for t in range(tiles):
        part = pl.ds(t * tile, tile)
        copy = pltpu.make_async_copy(cen_hbm.at[part], cen.at[part], cen_sem.at[t])
        copy.start()
        cen_copies.append(copy)

    pl.semaphore_wait(barrier, n - 1)

    odd = lax.rem(my_f, 2)
    partner = my_f + 1 - 2 * odd
    peers = [partner, lax.rem(my_f + 2, n_f), lax.rem(partner + 2, n_f)]
    slab_copies = []
    for c in range(chunks):
        copies = []
        for r, peer in enumerate(peers):
            at = pl.multiple_of(peer * rows_dev + c * crow, crow)
            copies.append(pltpu.make_async_remote_copy(
                src_ref=slab_hbm.at[:, pl.ds(at, crow)],
                dst_ref=points_ref.at[own_k, pl.ds(c * crow, crow)],
                send_sem=a_send.at[c, r], recv_sem=a_recv.at[c, r],
                device_id=(my_p, peer), device_id_type=MESH))
        slab_copies.append(copies)
    for copy in slab_copies[0][1:] + slab_copies[0][:1]:
        copy.start()

    for copy in in_copies[:4]:
        copy.wait()

    queries = n_p * SUB
    query_sub = lax.broadcasted_iota(jnp.int32, (queries, 1), 0)
    picked = jnp.full((queries, 1), -1, jnp.int32)
    for o in range(n_p):
        for s in range(slots):
            picked = jnp.where(query_sub == o * SUB + s, rows_ref[0, s, o], picked)
    members = labels_ref[...].astype(f32)
    lane_dev = lax.broadcasted_iota(jnp.int32, (queries, rows_dev), 1)
    own_hit = (lane_dev + my_f * rows_dev) == picked
    own_label = jnp.sum(jnp.where(own_hit, members + 1.0, 0.0), axis=1, keepdims=True)
    query_diag = (lax.broadcasted_iota(jnp.int32, (queries, LANES), 0)
                  == lax.broadcasted_iota(jnp.int32, (queries, LANES), 1))
    label_row = jnp.sum(jnp.where(query_diag, own_label, 0.0), axis=0, keepdims=True)
    lab_msg[...] = label_row
    lab_all[me] = label_row


    lab_copies = []
    for d in range(1, n):
        copy = pltpu.make_async_remote_copy(
            src_ref=lab_msg, dst_ref=lab_all.at[me], send_sem=lab_send.at[d - 1],
            recv_sem=lab_recv.at[d - 1], device_id=device(d), device_id_type=MESH)
        copy.start()
        lab_copies.append(copy)

    for copies in slab_copies[1:]:
        for copy in copies[1:] + copies[:1]:
            copy.start()
    for copy in in_copies[4:]:
        copy.wait()

    lane_pts = lax.broadcasted_iota(jnp.int32, (queries, rows_pts), 1)
    chosen = jnp.where(lane_pts == picked, 1.0, 0.0).astype(bf16)
    chosen = lax.dot_general(chosen, slab_ref[...], NT, preferred_element_type=f32)
    live = jnp.zeros((queries, 1), f32)
    for o in range(n_p):
        for s in range(slots):
            flag = jnp.where(count_ref[0, o] > s, 1.0, 0.0)
            live = jnp.where(query_sub == o * SUB + slots + s, flag, live)
    is_row = lax.rem(lax.broadcasted_iota(jnp.int32, (queries, width), 0), SUB) < slots
    sent = jnp.where(is_row, chosen, live)
    row_msg[:, :, :width] = sent.reshape(n_p, SUB, width)
    row_all[my_p] = row_msg[my_p]
    row_copies = []
    for d in range(1, n_p):
        owner = lax.rem(my_p + d, n_p)
        copy = pltpu.make_async_remote_copy(
            src_ref=row_msg.at[owner], dst_ref=row_all.at[my_p], send_sem=row_send.at[d - 1],
            recv_sem=row_recv.at[d - 1], device_id=(owner, my_f), device_id_type=MESH)
        copy.start()
        row_copies.append(copy)

    for t in range(tiles):
        cen_copies[t].wait()

    @pl.loop(0, tiles)
    def _(t):
        part = pl.ds(pl.multiple_of(t * tile, tile), tile)
        total = jnp.zeros((tile, LANES), f32)
        for b in range(cen.shape[1] // LANES):
            piece = cen[part, b * LANES:(b + 1) * LANES].astype(f32)
            total += piece * piece
        csq[part, :] = jnp.broadcast_to(jnp.sum(total, axis=1, keepdims=True), (tile, LANES))

    start = jnp.full((SUB, crow), jnp.inf, f32)

    def part_of(t):
        return pl.ds(pl.multiple_of(t * tile, tile), tile)

    def lower(best, gap):
        return jnp.minimum(best, jnp.min(gap.reshape(tile // SUB, SUB, crow), axis=0))

    def squares(part):
        return jnp.concatenate([csq[part, :]] * (crow // LANES), axis=1)

    def finish(best, cols):
        wide = points_ref[:, cols].astype(f32)
        return jnp.sum(wide * wide, axis=0, keepdims=True) + jnp.min(best, axis=0, keepdims=True)

    near_parts = []
    for c in range(chunks - 1):
        for copy in slab_copies[c]:
            copy.wait_recv()
        cols = pl.ds(c * crow, crow)
        points = points_ref[:, cols]

        def step(t, best):
            part = part_of(t)
            cross = jnp.dot(cen[part, :], points, preferred_element_type=f32)
            return lower(best, squares(part) - 2.0 * cross)

        near_parts.append(finish(lax.fori_loop(0, tiles, step, start), cols))

    for copy in lab_copies:
        copy.wait()
    lanes = lax.broadcasted_iota(jnp.int32, (queries, LANES), 1)
    slot = lax.rem(lax.broadcasted_iota(jnp.int32, (queries, LANES), 0), SUB)
    is_slot = slot < slots
    wanted = []
    sums = jnp.zeros((queries, LANES), f32)
    span = n_p * slots
    for p in range(n_p):
        row = lab_all[p * n_f]
        for g in range(1, n_f):
            row = row + lab_all[p * n_f + g]
        want = jnp.sum(jnp.where(query_diag, row, 0.0), axis=1, keepdims=True) - 1.0
        wanted.append(want)
        size = jnp.sum(jnp.where(want == members, 1.0, 0.0), axis=1, keepdims=True)
        sums = jnp.where(is_slot & (lanes == span + p * slots + slot), size, sums)

    pair = 2 * width
    last = pl.cdiv(width, LANES) * LANES
    here = my_f // 2
    away = 1 - here
    cols = pl.ds((chunks - 1) * crow, crow)
    here_k = pl.ds(pl.multiple_of(here * pair, LANES), pair)
    lone_k = pl.ds(pl.multiple_of(away * pair + odd * last, LANES), pair - last)
    last_k = pl.ds(pl.multiple_of(away * pair + (1 - odd) * (pair - last), LANES), last)
    for copy in slab_copies[-1][:2]:
        copy.wait_recv()
    first = jnp.concatenate([points_ref[here_k, cols], points_ref[lone_k, cols]], axis=0)

    @pl.loop(0, tiles)
    def _(t):
        part = part_of(t)
        mine = jnp.concatenate([cen[part, here_k], cen[part, lone_k]], axis=1)
        cross = jnp.dot(mine, first, preferred_element_type=f32)
        gap_ref[part, :] = squares(part) - 2.0 * cross

    slab_copies[-1][2].wait_recv()
    final = points_ref[last_k, cols]

    def last_step(t, best):
        part = part_of(t)
        cross = jnp.dot(cen[part, last_k], final, preferred_element_type=f32)
        return lower(best, gap_ref[part, :] - 2.0 * cross)

    near_parts.append(finish(lax.fori_loop(0, tiles, last_step, start), cols))
    nearest = jnp.concatenate(near_parts, axis=1)

    for p in range(n_p):
        cost = jnp.sum(jnp.where(wanted[p] == members, nearest, 0.0), axis=1, keepdims=True)
        sums = jnp.where(is_slot & (lanes == p * slots + slot), cost, sums)
    own_near = jnp.sum(jnp.where(own_hit, nearest, 0.0), axis=1, keepdims=True)
    sums = jnp.where(is_slot & (lanes == 2 * span + my_p * slots + slot), own_near, sums)
    to_owner = jnp.sum(jnp.where(is_slot, sums, 0.0).reshape(n_p, SUB, LANES), axis=1, keepdims=True)
    red_msg[...] = to_owner
    red_all[0] = red_msg[my_p]
    red_copies = []
    for d in range(1, n):
        to = device(d)
        copy = pltpu.make_async_remote_copy(
            src_ref=red_msg.at[to[0]], dst_ref=red_all.at[d], send_sem=red_send.at[d - 1],
            recv_sem=red_recv.at[d - 1], device_id=to, device_id_type=MESH)
        copy.start()
        red_copies.append(copy)
    for copy in row_copies:
        copy.wait()
    for copies in slab_copies:
        for copy in copies:
            copy.wait_send()
    for copy in red_copies:
        copy.wait()
    total = jnp.broadcast_to(jnp.sum(red_all[...], axis=0), (SUB, LANES))
    size = pltpu.roll(total, LANES - span, 1)
    near = pltpu.roll(total, LANES - 2 * span, 1)
    weight = (2.0 * centre_count / (rows_pts * n_p)) / (near / total + 1.0 / size)
    sub = lax.broadcasted_iota(jnp.int32, (SUB, LANES), 0)
    lane = lax.broadcasted_iota(jnp.int32, (SUB, LANES), 1)
    out_rows = out_ref.shape[0]
    out_iota = lax.broadcasted_iota(jnp.int32, (out_rows, width), 0)
    placed = jnp.zeros((out_rows, width), f32)
    for p in range(n_p):
        mine = (sub < slots) & (lane == p * slots + sub)
        factor = jnp.sum(jnp.where(mine, weight, 0.0), axis=1, keepdims=True)
        block = row_all[p][:, :width]
        scaled = (block * factor).astype(bf16).astype(f32)
        for s in range(slots):
            flag = block[slots + s:slots + s + 1] > 0.5
            hit = (out_iota == offset_ref[0, p] + s) & flag
            placed = jnp.where(hit, scaled[s:s + 1], placed)
    out_ref[...] = placed.astype(bf16)


def fused(n_p, n_f, slab, centres, labels, sample_rows, sample_count, slot_offset):
    rows_pts, width = slab.shape
    rows_dev = rows_pts // n_f
    centre_count, depth = centres.shape
    slots = sample_rows.shape[2]
    chunks = rows_dev // CHUNK
    tiles = centre_count // TILE
    n = n_p * n_f
    wide = pl.cdiv(width, LANES) * LANES
    rows_in = sample_rows.transpose(0, 2, 1)
    labels_in = labels.reshape(1, -1)
    dma = pltpu.SemaphoreType.DMA
    return pl.pallas_call(
        functools.partial(kernel, n_p, n_f, chunks, TILE),
        out_shape=pltpu.VMEM((n_p * slots, width), jnp.bfloat16),
        in_specs=[pl.BlockSpec(memory_space=pl.ANY)] * 6,
        out_specs=pl.BlockSpec(memory_space=pltpu.VMEM),
        scratch_shapes=[
            pltpu.VMEM((centre_count, depth), jnp.bfloat16),
            pltpu.VMEM((centre_count, LANES), jnp.float32),
            pltpu.VMEM((centre_count, CHUNK), jnp.float32),
            pltpu.VMEM((width, rows_pts), jnp.bfloat16),
            pltpu.VMEM((depth, rows_dev), jnp.bfloat16),
            pltpu.VMEM(labels_in.shape, jnp.int32),
            pltpu.SMEM(rows_in.shape, jnp.int32),
            pltpu.SMEM(sample_count.shape, jnp.int32),
            pltpu.SMEM(slot_offset.shape, jnp.int32),
            pltpu.VMEM((1, LANES), jnp.float32),
            pltpu.VMEM((n, 1, LANES), jnp.float32),
            pltpu.VMEM((n_p, SUB, wide), jnp.float32),
            pltpu.VMEM((n_p, SUB, wide), jnp.float32),
            pltpu.VMEM((n_p, 1, LANES), jnp.float32),
            pltpu.VMEM((n, 1, LANES), jnp.float32),
            dma((6,)), dma((tiles,)),
            dma((chunks, n_f - 1)), dma((chunks, n_f - 1)),
            dma((n - 1,)), dma((n - 1,)),
            dma((n_p - 1,)), dma((n_p - 1,)),
            dma((n - 1,)), dma((n - 1,)),
        ],
        compiler_params=pltpu.CompilerParams(collective_id=0, has_side_effects=True),
    )(slab.T, labels_in, rows_in, sample_count, slot_offset, centres)


def solution(mesh):
    n_p, n_f = mesh.shape["pts"], mesh.shape["feat"]

    def body(slab, centres, labels, sample_rows, sample_count, slot_offset):
        rows_dev = slab.shape[0] // n_f
        slots = sample_rows.shape[2]
        fits = (
            slab.shape[1] % 16 == 0 and rows_dev % CHUNK == 0 and centres.shape[0] % TILE == 0
            and n_f == 4 and 2 * slab.shape[1] % LANES == 0 and slab.shape[1] > LANES and rows_dev // CHUNK > 1
            and 3 * n_p * slots <= LANES and n_p * SUB <= LANES and 2 * slots <= SUB
        )
        args = (slab, centres, labels, sample_rows, sample_count, slot_offset)
        return fused(n_p, n_f, *args) if fits else local(*args)

    placed = (
        P("pts", "feat"),
        P(),
        P(("pts", "feat"), None),
        P("pts", None, None),
        P("pts", None),
        P("pts", None),
    )
    return jax.shard_map(
        body, mesh=mesh, in_specs=placed, out_specs=P("pts", "feat"), check_vma=False
    )
```

```python
import functools

import jax
import jax.numpy as jnp
from jax import lax
from jax.experimental import pallas as pl
from jax.experimental.pallas import tpu as pltpu
from jax.sharding import PartitionSpec as P

NT = (((1,), (1,)), ((), ()))
LANES = 128
SUB = 8
CHUNK = 256
TILE = 2048
MESH = pl.DeviceIdType.MESH


def local(slab, centres, labels, sample_rows, sample_count, slot_offset):
    rows_pts, feat_width = slab.shape
    feat_count = lax.axis_size("feat")
    rows_dev = rows_pts // feat_count
    centre_count = centres.shape[0]
    centre_sq = jnp.sum(jnp.square(centres.astype(jnp.float32)), axis=1)
    stacked = slab.reshape(feat_count, rows_dev, feat_width)
    points = lax.all_to_all(stacked, "feat", split_axis=0, concat_axis=2, tiled=True)[0]
    cross_term = lax.dot_general(points, centres, NT, preferred_element_type=jnp.float32)
    point_sq = jnp.sum(jnp.square(points.astype(jnp.float32)), axis=1)
    nearest = jnp.min(point_sq[:, None] + centre_sq[None, :] - 2.0 * cross_term, axis=1)[None, :][0]
    member = labels[:, 0]
    cost_part = jax.ops.segment_sum(nearest, member, num_segments=centre_count)
    size_part = jax.ops.segment_sum(jnp.ones_like(nearest), member, num_segments=centre_count)
    cluster_cost, cluster_size = lax.psum((cost_part, size_part), ("pts", "feat"))
    own_sens = nearest / jnp.take(cluster_cost, member) + 1.0 / jnp.take(cluster_size, member)
    shard_sens = lax.all_gather(own_sens, "feat", axis=0, tiled=True)
    total_points = rows_pts * lax.axis_size("pts")
    weight = 2.0 * centre_count / total_points / shard_sens
    picked_rows = sample_rows[0]
    owner_count, slot_count = picked_rows.shape
    chosen = jnp.take(slab, picked_rows.reshape(-1), axis=0).reshape(
        owner_count, slot_count, feat_width
    )
    chosen_weight = jnp.take(weight, picked_rows)
    live_slot = jnp.arange(slot_count, dtype=jnp.int32)[None, :] < sample_count[0][:, None]
    scaled = jnp.where(
        live_slot[:, :, None], chosen.astype(jnp.float32) * chosen_weight[:, :, None], 0.0
    ).astype(jnp.bfloat16)
    arrived = lax.all_to_all(scaled, "pts", split_axis=0, concat_axis=0, tiled=True)
    target = slot_offset[0][:, None] + jnp.arange(slot_count, dtype=jnp.int32)[None, :]
    own_rows = arrived.shape[0] * slot_count
    placed = jnp.zeros((own_rows, feat_width), jnp.float32)
    placed = placed.at[target.reshape(-1)].add(
        arrived.reshape(-1, feat_width).astype(jnp.float32), mode="drop"
    )
    return placed.astype(jnp.bfloat16)


def kernel(n_p, n_f, chunks, tile, slab_hbm, labels_hbm, rows_hbm, count_hbm, offset_hbm, cen_hbm,
           out_ref, cen, csq, gap_ref, slab_ref, points_ref, labels_ref, rows_ref, count_ref, offset_ref,
           part_msg, part_all, lab_msg, lab_all, wide_lab, hot, row_msg, row_all, red_msg, red_all,
           in_sem, cen_sem, a_send, a_recv, part_send, part_recv, lab_send, lab_recv, row_send, row_recv,
           red_send, red_recv, hop_sem, pair_sem, feat_sem):
    f32, bf16 = jnp.float32, jnp.bfloat16
    width, rows_pts = slab_ref.shape
    rows_dev = rows_pts // n_f
    crow = rows_dev // chunks
    n = n_p * n_f
    centre_count = cen.shape[0]
    slots = rows_ref.shape[1]
    span = n_p * slots
    tiles = centre_count // tile
    my_p, my_f = lax.axis_index("pts"), lax.axis_index("feat")
    me = my_p * n_f + my_f

    def device(d):
        other = lax.rem(me + d, n)
        return other // n_f, lax.rem(other, n_f)

    def tell(sem, where):
        pl.semaphore_signal(sem, inc=1, device_id=where, device_id_type=MESH)

    odd = lax.rem(my_f, 2)
    partner = my_f + 1 - 2 * odd
    peers = [partner, lax.rem(my_f + 2, n_f), lax.rem(partner + 2, n_f)]
    twin = my_p + 1 - 2 * lax.rem(my_p, 2)
    has_down, has_up = my_p >= 2, my_p < n_p - 2
    links = jnp.where(has_down, 1, 0) + jnp.where(has_up, 1, 0)

    def tell_chain(sem):
        @pl.when(has_down)
        def _():
            tell(sem, (my_p - 2, my_f))

        @pl.when(has_up)
        def _():
            tell(sem, (my_p + 2, my_f))

    barrier = pltpu.get_barrier_semaphore()
    for peer in peers[1:] + peers[:1]:
        tell(barrier, (my_p, peer))
    tell(barrier, (twin, my_f))
    tell_chain(barrier)

    own_k = pl.ds(pl.multiple_of(my_f * width, width), width)
    own_cols = pl.ds(pl.multiple_of(my_f * rows_dev, rows_dev), rows_dev)
    in_copies = [
        pltpu.make_async_copy(rows_hbm, rows_ref, in_sem.at[0]),
        pltpu.make_async_copy(labels_hbm, labels_ref, in_sem.at[1]),
        pltpu.make_async_copy(count_hbm, count_ref, in_sem.at[2]),
        pltpu.make_async_copy(offset_hbm, offset_ref, in_sem.at[3]),
        pltpu.make_async_copy(slab_hbm, slab_ref, in_sem.at[4]),
        pltpu.make_async_copy(slab_hbm.at[:, own_cols], points_ref.at[own_k], in_sem.at[5]),
    ]
    for copy in in_copies:
        copy.start()
    cen_copies = []
    for t in range(tiles):
        part = pl.ds(t * tile, tile)
        copy = pltpu.make_async_copy(cen_hbm.at[part], cen.at[part], cen_sem.at[t])
        copy.start()
        cen_copies.append(copy)

    pl.semaphore_wait(barrier, n_f + links)

    slab_copies = []
    for c in range(chunks):
        copies = []
        for r, peer in enumerate(peers):
            at = pl.multiple_of(peer * rows_dev + c * crow, crow)
            copies.append(pltpu.make_async_remote_copy(
                src_ref=slab_hbm.at[:, pl.ds(at, crow)],
                dst_ref=points_ref.at[own_k, pl.ds(c * crow, crow)],
                send_sem=a_send.at[c, r], recv_sem=a_recv.at[c, r],
                device_id=(my_p, peer), device_id_type=MESH))
        slab_copies.append(copies)
    for c, r in [(0, 1), (0, 0)] + [(c, 0) for c in range(1, chunks)]:
        slab_copies[c][r].start()

    rounds = n_p // 2 - 2
    if rounds:
        tell_chain(hop_sem.at[0])

    for copy in in_copies[:2]:
        copy.wait()
    queries = n_p * SUB
    query_sub = lax.broadcasted_iota(jnp.int32, (queries, 1), 0)
    picked = jnp.full((queries, 1), -1, jnp.int32)
    for o in range(n_p):
        for s in range(slots):
            picked = jnp.where(query_sub == o * SUB + s, rows_ref[0, s, o], picked)
    members = labels_ref[...].astype(f32)
    lane_dev = lax.broadcasted_iota(jnp.int32, (queries, rows_dev), 1)
    own_hit = (lane_dev + my_f * rows_dev) == picked
    own_label = jnp.sum(jnp.where(own_hit, members + 1.0, 0.0), axis=1, keepdims=True)
    lane_q = lax.broadcasted_iota(jnp.int32, (queries, LANES), 1)
    sub_q = lax.broadcasted_iota(jnp.int32, (queries, LANES), 0)
    to_lane = (lax.rem(sub_q, SUB) < slots) & (lane_q == sub_q // SUB * slots + lax.rem(sub_q, SUB))
    part_msg[...] = jnp.sum(jnp.where(to_lane, own_label, 0.0), axis=0, keepdims=True)
    part_copies = []
    for r, peer in enumerate(peers):
        copy = pltpu.make_async_remote_copy(
            src_ref=part_msg, dst_ref=part_all.at[r], send_sem=part_send.at[r],
            recv_sem=part_recv.at[r], device_id=(my_p, peer), device_id_type=MESH)
        copy.start()
        part_copies.append(copy)
    for c, r in [(0, 2)] + [(c, r) for c in range(1, chunks) for r in (1, 2)]:
        slab_copies[c][r].start()

    for k in range(rounds):
        pl.semaphore_wait(hop_sem.at[k], links)
        if k + 1 < rounds:
            tell_chain(hop_sem.at[k + 1])
    tell(pair_sem.at[0], (twin, my_f))

    for copy in in_copies[2:]:
        copy.wait()
    lane_pts = lax.broadcasted_iota(jnp.int32, (queries, rows_pts), 1)
    chosen = jnp.where(lane_pts == picked, 1.0, 0.0).astype(bf16)
    chosen = lax.dot_general(chosen, slab_ref[...], NT, preferred_element_type=f32)
    live = jnp.zeros((queries, 1), f32)
    for o in range(n_p):
        for s in range(slots):
            flag = jnp.where(count_ref[0, o] > s, 1.0, 0.0)
            live = jnp.where(query_sub == o * SUB + slots + s, flag, live)
    is_row = lax.rem(lax.broadcasted_iota(jnp.int32, (queries, width), 0), SUB) < slots
    sent = jnp.where(is_row, chosen, live)
    row_msg[:, :, :width] = sent.reshape(n_p, SUB, width)
    row_all[my_p] = row_msg[my_p]

    pl.semaphore_wait(pair_sem.at[0], 1)
    for peer in peers[1:] + peers[:1]:
        tell(feat_sem.at[0], (my_p, peer))

    row_copies = []
    for d in range(1, n_p):
        owner = lax.rem(my_p + d, n_p)
        copy = pltpu.make_async_remote_copy(
            src_ref=row_msg.at[owner], dst_ref=row_all.at[my_p], send_sem=row_send.at[d - 1],
            recv_sem=row_recv.at[d - 1], device_id=(owner, my_f), device_id_type=MESH)
        copy.start()
        row_copies.append(copy)

    for t in range(tiles):
        cen_copies[t].wait()

    @pl.loop(0, tiles)
    def _(t):
        part = pl.ds(pl.multiple_of(t * tile, tile), tile)
        total = jnp.zeros((tile, LANES), f32)
        for b in range(cen.shape[1] // LANES):
            piece = cen[part, b * LANES:(b + 1) * LANES].astype(f32)
            total += piece * piece
        csq[part, :] = jnp.broadcast_to(0.5 * jnp.sum(total, axis=1, keepdims=True), (tile, LANES))

    for copy in part_copies:
        copy.wait()
    label_row = part_msg[...]
    for r in range(n_f - 1):
        label_row = label_row + part_all[r]
    lab_msg[...] = label_row
    lab_all[my_p] = label_row
    lab_copies = []
    for d in range(1, n_p):
        copy = pltpu.make_async_remote_copy(
            src_ref=lab_msg, dst_ref=lab_all.at[my_p], send_sem=lab_send.at[d - 1],
            recv_sem=lab_recv.at[d - 1], device_id=(lax.rem(my_p + d, n_p), my_f), device_id_type=MESH)
        copy.start()
        lab_copies.append(copy)

    start = jnp.full((SUB, crow), jnp.inf, f32)

    def part_of(t):
        return pl.ds(pl.multiple_of(t * tile, tile), tile)

    def lower(best, gap):
        return jnp.minimum(best, jnp.min(gap.reshape(tile // SUB, SUB, crow), axis=0))

    def squares(part):
        return jnp.concatenate([csq[part, :]] * (crow // LANES), axis=1)

    def norm(piece):
        wide = piece.astype(f32)
        return jnp.sum(wide * wide, axis=0, keepdims=True)

    def finish(best, point_sq):
        return point_sq + 2.0 * jnp.min(best, axis=0, keepdims=True)

    pair = 2 * width
    last = pl.cdiv(width, LANES) * LANES
    here = my_f // 2
    away = 1 - here
    here_k = pl.ds(pl.multiple_of(here * pair, LANES), pair)
    lone_k = pl.ds(pl.multiple_of(away * pair + odd * last, LANES), pair - last)
    last_k = pl.ds(pl.multiple_of(away * pair + (1 - odd) * (pair - last), LANES), last)

    def open_chunk(c):
        for copy in slab_copies[c][:2]:
            copy.wait_recv()
        cols = pl.ds(c * crow, crow)
        first = jnp.concatenate([points_ref[here_k, cols], points_ref[lone_k, cols]], axis=0)

        @pl.loop(0, tiles)
        def _(t):
            part = part_of(t)
            mine = jnp.concatenate([cen[part, here_k], cen[part, lone_k]], axis=1)
            cross = jnp.dot(mine, first, preferred_element_type=f32)
            gap_ref[part, :] = squares(part) - cross

        return norm(first)

    def close_chunk(c, first_sq):
        slab_copies[c][2].wait_recv()
        final = points_ref[last_k, pl.ds(c * crow, crow)]
        point_sq = first_sq + norm(final)

        def last_step(t, best):
            part = part_of(t)
            cross = jnp.dot(cen[part, last_k], final, preferred_element_type=f32)
            return lower(best, gap_ref[part, :] - cross)

        return finish(lax.fori_loop(0, tiles, last_step, start), point_sq)

    near_parts = [close_chunk(c, open_chunk(c)) for c in range(chunks - 1)]

    for copy in lab_copies:
        copy.wait()
    for p in range(n_p):
        wide_lab[p * slots:(p + 1) * slots, :] = jnp.broadcast_to(lab_all[p], (slots, LANES))
    wide = wide_lab[...]
    lane_s = lax.broadcasted_iota(jnp.int32, (span, LANES), 1)
    sub_s = lax.broadcasted_iota(jnp.int32, (span, LANES), 0)
    lane_w = lax.broadcasted_iota(jnp.int32, (span, rows_dev), 1) + my_f * rows_dev
    sub_w = lax.broadcasted_iota(jnp.int32, (span, 1), 0)
    for o in range(n_p):
        want = jnp.sum(jnp.where(lane_s == o * slots + lax.rem(sub_s, slots), wide, 0.0),
                       axis=1, keepdims=True) - 1.0
        pick = jnp.full((span, 1), -1, jnp.int32)
        for s in range(slots):
            pick = jnp.where(sub_w == my_p * slots + s, rows_ref[0, s, o], pick)
        hot[o * LANES:o * LANES + span] = jnp.where(want == members, 1.0, 0.0).astype(bf16)
        hot[o * LANES + span:o * LANES + 2 * span] = jnp.where(pick == lane_w, 1.0, 0.0).astype(bf16)
        hot[o * LANES + 2 * span:(o + 1) * LANES] = jnp.zeros((LANES - 2 * span, rows_dev), bf16)

    def summed(values, cols):
        high = values.astype(bf16).astype(f32)
        rest = values - high
        middle = rest.astype(bf16).astype(f32)
        terms = jnp.concatenate([high, middle, rest - middle] + [jnp.ones_like(high)] * 5, axis=0)
        return lax.dot_general(terms.astype(bf16), hot[:, cols], NT, preferred_element_type=f32)

    early = jnp.concatenate(near_parts, axis=1)
    done = summed(early, pl.ds(0, early.shape[1]))
    lane_n = lax.broadcasted_iota(jnp.int32, (1, n_p * LANES), 1)
    later = summed(jnp.zeros((1, crow), f32), pl.ds((chunks - 1) * crow, crow))
    sizes = done[3:4] + later[3:4]
    is_cost = lax.rem(lane_n, LANES) < span
    begun = done[0:1] + done[1:2] + done[2:3] + pltpu.roll(jnp.where(is_cost, sizes, 0.0), 2 * span, 1)

    for copy in row_copies:
        copy.wait()
    sub = lax.broadcasted_iota(jnp.int32, (out_ref.shape[0], LANES), 0)
    lane = lax.broadcasted_iota(jnp.int32, (out_ref.shape[0], LANES), 1)
    out_iota = lax.broadcasted_iota(jnp.int32, out_ref.shape, 0)
    placed = jnp.zeros(out_ref.shape, f32)
    spread = jnp.zeros((out_ref.shape[0], LANES), f32)
    for p in range(n_p):
        block = row_all[p][:, :width]
        for s in range(slots):
            flag = block[slots + s:slots + s + 1] > 0.5
            at = offset_ref[0, p] + s
            placed = jnp.where((out_iota == at) & flag, block[s:s + 1], placed)
            spread = jnp.where((sub == at) & (lane == p * slots + s) & flag[:, :LANES], 1.0, spread)

    first_sq = open_chunk(chunks - 1)
    pl.semaphore_wait(feat_sem.at[0], n_f - 1)
    nearest = close_chunk(chunks - 1, first_sq)
    tail = summed(nearest, pl.ds((chunks - 1) * crow, crow))
    total = begun + tail[0:1] + tail[1:2] + tail[2:3]
    for o in range(n_p):
        red_msg[o] = total[:, o * LANES:(o + 1) * LANES]
    red_all[0] = red_msg[my_p]
    red_copies = []
    for d in range(1, n):
        to = device(d)
        copy = pltpu.make_async_remote_copy(
            src_ref=red_msg.at[to[0]], dst_ref=red_all.at[d], send_sem=red_send.at[d - 1],
            recv_sem=red_recv.at[0], device_id=to, device_id_type=MESH)
        copy.start()
        red_copies.append(copy)
    for copies in slab_copies:
        for copy in copies:
            copy.wait_send()
    for copy in red_copies:
        copy.wait_send()
    pltpu.make_async_remote_copy(
        src_ref=red_all.at[pl.ds(0, n - 1)], dst_ref=red_all.at[pl.ds(1, n - 1)], send_sem=red_send.at[0],
        recv_sem=red_recv.at[0], device_id=device(1), device_id_type=MESH).wait_recv()
    total = jnp.sum(red_all[...], axis=0)
    near = pltpu.roll(total, LANES - span, 1)
    size = pltpu.roll(total, LANES - 2 * span, 1)
    weight = (2.0 * centre_count / (rows_pts * n_p)) / (near / total + 1.0 / size)
    factor = jnp.sum(jnp.where(spread > 0.5, weight, 0.0), axis=1, keepdims=True)
    out_ref[...] = (placed * factor).astype(bf16)


def fused(n_p, n_f, slab, centres, labels, sample_rows, sample_count, slot_offset):
    rows_pts, width = slab.shape
    rows_dev = rows_pts // n_f
    centre_count, depth = centres.shape
    slots = sample_rows.shape[2]
    chunks = rows_dev // CHUNK
    tiles = centre_count // TILE
    n = n_p * n_f
    wide = pl.cdiv(width, LANES) * LANES
    rows_in = sample_rows.transpose(0, 2, 1)
    labels_in = labels.reshape(1, -1)
    dma, regular = pltpu.SemaphoreType.DMA, pltpu.SemaphoreType.REGULAR
    return pl.pallas_call(
        functools.partial(kernel, n_p, n_f, chunks, TILE),
        out_shape=pltpu.VMEM((n_p * slots, width), jnp.bfloat16),
        in_specs=[pl.BlockSpec(memory_space=pl.ANY)] * 6,
        out_specs=pl.BlockSpec(memory_space=pltpu.VMEM),
        scratch_shapes=[
            pltpu.VMEM((centre_count, depth), jnp.bfloat16),
            pltpu.VMEM((centre_count, LANES), jnp.float32),
            pltpu.VMEM((centre_count, CHUNK), jnp.float32),
            pltpu.VMEM((width, rows_pts), jnp.bfloat16),
            pltpu.VMEM((depth, rows_dev), jnp.bfloat16),
            pltpu.VMEM(labels_in.shape, jnp.int32),
            pltpu.SMEM(rows_in.shape, jnp.int32),
            pltpu.SMEM(sample_count.shape, jnp.int32),
            pltpu.SMEM(slot_offset.shape, jnp.int32),
            pltpu.VMEM((1, LANES), jnp.float32),
            pltpu.VMEM((n_f - 1, 1, LANES), jnp.float32),
            pltpu.VMEM((1, LANES), jnp.float32),
            pltpu.VMEM((n_p, 1, LANES), jnp.float32),
            pltpu.VMEM((n_p * slots, LANES), jnp.float32),
            pltpu.VMEM((n_p * LANES, rows_dev), jnp.bfloat16),
            pltpu.VMEM((n_p, SUB, wide), jnp.float32),
            pltpu.VMEM((n_p, SUB, wide), jnp.float32),
            pltpu.VMEM((n_p, 1, LANES), jnp.float32),
            pltpu.VMEM((n, 1, LANES), jnp.float32),
            dma((6,)), dma((tiles,)),
            dma((chunks, n_f - 1)), dma((chunks, n_f - 1)),
            dma((n_f - 1,)), dma((n_f - 1,)),
            dma((n_p - 1,)), dma((n_p - 1,)),
            dma((n_p - 1,)), dma((n_p - 1,)),
            dma((n - 1,)), dma((1,)),
            regular((max(n_p // 2 - 2, 1),)), regular((1,)), regular((1,)),
        ],
        compiler_params=pltpu.CompilerParams(collective_id=0, has_side_effects=True),
    )(slab.T, labels_in, rows_in, sample_count, slot_offset, centres)


def solution(mesh):
    n_p, n_f = mesh.shape["pts"], mesh.shape["feat"]

    def body(slab, centres, labels, sample_rows, sample_count, slot_offset):
        rows_dev = slab.shape[0] // n_f
        slots = sample_rows.shape[2]
        fits = (
            slab.shape[1] % 16 == 0 and rows_dev % CHUNK == 0 and centres.shape[0] % TILE == 0
            and n_f == 4 and 2 * slab.shape[1] % LANES == 0 and slab.shape[1] > LANES and rows_dev // CHUNK > 1
            and 3 * n_p * slots <= LANES and 2 * slots <= SUB and n_p % 2 == 0 and n_p > 2 and n_p * slots % 16 == 0
        )
        args = (slab, centres, labels, sample_rows, sample_count, slot_offset)
        return fused(n_p, n_f, *args) if fits else local(*args)

    placed = (
        P("pts", "feat"),
        P(),
        P(("pts", "feat"), None),
        P("pts", None, None),
        P("pts", None),
        P("pts", None),
    )
    return jax.shard_map(
        body, mesh=mesh, in_specs=placed, out_specs=P("pts", "feat"), check_vma=False
    )
```

```python
import functools

import jax
import jax.numpy as jnp
from jax import lax
from jax.experimental import pallas as pl
from jax.experimental.pallas import tpu as pltpu
from jax.sharding import PartitionSpec as P

NT = (((1,), (1,)), ((), ()))
LANES = 128
SUB = 8
CHUNK = 256
TILE = 2048
STEP = 512
MESH = pl.DeviceIdType.MESH


def local(slab, centres, labels, sample_rows, sample_count, slot_offset):
    rows_pts, feat_width = slab.shape
    feat_count = lax.axis_size("feat")
    rows_dev = rows_pts // feat_count
    centre_count = centres.shape[0]
    centre_sq = jnp.sum(jnp.square(centres.astype(jnp.float32)), axis=1)
    stacked = slab.reshape(feat_count, rows_dev, feat_width)
    points = lax.all_to_all(stacked, "feat", split_axis=0, concat_axis=2, tiled=True)[0]
    cross_term = lax.dot_general(points, centres, NT, preferred_element_type=jnp.float32)
    point_sq = jnp.sum(jnp.square(points.astype(jnp.float32)), axis=1)
    nearest = jnp.min(point_sq[:, None] + centre_sq[None, :] - 2.0 * cross_term, axis=1)[None, :][0]
    member = labels[:, 0]
    cost_part = jax.ops.segment_sum(nearest, member, num_segments=centre_count)
    size_part = jax.ops.segment_sum(jnp.ones_like(nearest), member, num_segments=centre_count)
    cluster_cost, cluster_size = lax.psum((cost_part, size_part), ("pts", "feat"))
    own_sens = nearest / jnp.take(cluster_cost, member) + 1.0 / jnp.take(cluster_size, member)
    shard_sens = lax.all_gather(own_sens, "feat", axis=0, tiled=True)
    total_points = rows_pts * lax.axis_size("pts")
    weight = 2.0 * centre_count / total_points / shard_sens
    picked_rows = sample_rows[0]
    owner_count, slot_count = picked_rows.shape
    chosen = jnp.take(slab, picked_rows.reshape(-1), axis=0).reshape(
        owner_count, slot_count, feat_width
    )
    chosen_weight = jnp.take(weight, picked_rows)
    live_slot = jnp.arange(slot_count, dtype=jnp.int32)[None, :] < sample_count[0][:, None]
    scaled = jnp.where(
        live_slot[:, :, None], chosen.astype(jnp.float32) * chosen_weight[:, :, None], 0.0
    ).astype(jnp.bfloat16)
    arrived = lax.all_to_all(scaled, "pts", split_axis=0, concat_axis=0, tiled=True)
    target = slot_offset[0][:, None] + jnp.arange(slot_count, dtype=jnp.int32)[None, :]
    own_rows = arrived.shape[0] * slot_count
    placed = jnp.zeros((own_rows, feat_width), jnp.float32)
    placed = placed.at[target.reshape(-1)].add(
        arrived.reshape(-1, feat_width).astype(jnp.float32), mode="drop"
    )
    return placed.astype(jnp.bfloat16)


def kernel(n_p, n_f, chunks, tile, slab_hbm, labels_hbm, rows_hbm, count_hbm, offset_hbm, cen_hbm,
           out_ref, cen, csq, gap_ref, slab_ref, points_ref, labels_ref, rows_ref, count_ref, offset_ref,
           part_msg, part_all, lab_msg, lab_all, wide_lab, hot, row_msg, row_all, red_msg, red_all,
           in_sem, cen_sem, a_send, a_recv, part_send, part_recv, lab_send, lab_recv, row_send, row_recv,
           red_send, red_recv, hop_sem, pair_sem, feat_sem):
    f32, bf16 = jnp.float32, jnp.bfloat16
    width, rows_pts = slab_ref.shape
    rows_dev = rows_pts // n_f
    crow = rows_dev // chunks
    n = n_p * n_f
    centre_count = cen.shape[0]
    slots = rows_ref.shape[1]
    span = n_p * slots
    tiles = centre_count // tile
    my_p, my_f = lax.axis_index("pts"), lax.axis_index("feat")
    me = my_p * n_f + my_f

    def device(d):
        other = lax.rem(me + d, n)
        return other // n_f, lax.rem(other, n_f)

    def tell(sem, where):
        pl.semaphore_signal(sem, inc=1, device_id=where, device_id_type=MESH)

    odd = lax.rem(my_f, 2)
    partner = my_f + 1 - 2 * odd
    peers = [partner, lax.rem(my_f + 2, n_f), lax.rem(partner + 2, n_f)]
    twin = my_p + 1 - 2 * lax.rem(my_p, 2)
    has_down, has_up = my_p >= 2, my_p < n_p - 2
    links = jnp.where(has_down, 1, 0) + jnp.where(has_up, 1, 0)

    def tell_chain(sem):
        @pl.when(has_down)
        def _():
            tell(sem, (my_p - 2, my_f))

        @pl.when(has_up)
        def _():
            tell(sem, (my_p + 2, my_f))

    barrier = pltpu.get_barrier_semaphore()
    for peer in peers[1:] + peers[:1]:
        tell(barrier, (my_p, peer))
    tell(barrier, (twin, my_f))
    tell_chain(barrier)

    own_k = pl.ds(pl.multiple_of(my_f * width, width), width)
    own_cols = pl.ds(pl.multiple_of(my_f * rows_dev, rows_dev), rows_dev)
    in_copies = [
        pltpu.make_async_copy(rows_hbm, rows_ref, in_sem.at[0]),
        pltpu.make_async_copy(labels_hbm, labels_ref, in_sem.at[1]),
        pltpu.make_async_copy(count_hbm, count_ref, in_sem.at[2]),
        pltpu.make_async_copy(offset_hbm, offset_ref, in_sem.at[3]),
        pltpu.make_async_copy(slab_hbm, slab_ref, in_sem.at[4]),
        pltpu.make_async_copy(slab_hbm.at[:, own_cols], points_ref.at[own_k], in_sem.at[5]),
    ]
    for copy in in_copies:
        copy.start()
    cen_copies = []
    for t in range(tiles):
        part = pl.ds(t * tile, tile)
        copy = pltpu.make_async_copy(cen_hbm.at[part], cen.at[part], cen_sem.at[t])
        copy.start()
        cen_copies.append(copy)

    pl.semaphore_wait(barrier, n_f + links)

    slab_copies = []
    for c in range(chunks):
        copies = []
        for r, peer in enumerate(peers):
            at = pl.multiple_of(peer * rows_dev + c * crow, crow)
            copies.append(pltpu.make_async_remote_copy(
                src_ref=slab_hbm.at[:, pl.ds(at, crow)],
                dst_ref=points_ref.at[own_k, pl.ds(c * crow, crow)],
                send_sem=a_send.at[c, r], recv_sem=a_recv.at[c, r],
                device_id=(my_p, peer), device_id_type=MESH))
        slab_copies.append(copies)
    for c, r in [(0, 1), (0, 0)] + [(c, 0) for c in range(1, chunks)]:
        slab_copies[c][r].start()

    rounds = n_p // 2 - 2
    if rounds:
        tell_chain(hop_sem.at[0])

    for copy in in_copies[:2]:
        copy.wait()
    queries = n_p * SUB
    query_sub = lax.broadcasted_iota(jnp.int32, (queries, 1), 0)
    picked = jnp.full((queries, 1), -1, jnp.int32)
    for o in range(n_p):
        for s in range(slots):
            picked = jnp.where(query_sub == o * SUB + s, rows_ref[0, s, o], picked)
    members = labels_ref[...].astype(f32)
    lane_dev = lax.broadcasted_iota(jnp.int32, (queries, rows_dev), 1)
    own_hit = (lane_dev + my_f * rows_dev) == picked
    own_label = jnp.sum(jnp.where(own_hit, members + 1.0, 0.0), axis=1, keepdims=True)
    lane_q = lax.broadcasted_iota(jnp.int32, (queries, LANES), 1)
    sub_q = lax.broadcasted_iota(jnp.int32, (queries, LANES), 0)
    to_lane = (lax.rem(sub_q, SUB) < slots) & (lane_q == sub_q // SUB * slots + lax.rem(sub_q, SUB))
    part_msg[...] = jnp.sum(jnp.where(to_lane, own_label, 0.0), axis=0, keepdims=True)
    part_copies = []
    for r, peer in enumerate(peers):
        copy = pltpu.make_async_remote_copy(
            src_ref=part_msg, dst_ref=part_all.at[r], send_sem=part_send.at[r],
            recv_sem=part_recv.at[r], device_id=(my_p, peer), device_id_type=MESH)
        copy.start()
        part_copies.append(copy)
    for c, r in [(0, 2)] + [(c, r) for c in range(1, chunks) for r in (1, 2)]:
        slab_copies[c][r].start()

    for k in range(rounds):
        pl.semaphore_wait(hop_sem.at[k], links)
        if k + 1 < rounds:
            tell_chain(hop_sem.at[k + 1])
    tell(pair_sem.at[0], (twin, my_f))

    for copy in in_copies[2:]:
        copy.wait()
    lane_pts = lax.broadcasted_iota(jnp.int32, (queries, rows_pts), 1)
    chosen = jnp.where(lane_pts == picked, 1.0, 0.0).astype(bf16)
    chosen = lax.dot_general(chosen, slab_ref[...], NT, preferred_element_type=f32)
    live = jnp.zeros((queries, 1), f32)
    for o in range(n_p):
        for s in range(slots):
            flag = jnp.where(count_ref[0, o] > s, 1.0, 0.0)
            live = jnp.where(query_sub == o * SUB + slots + s, flag, live)
    is_row = lax.rem(lax.broadcasted_iota(jnp.int32, (queries, width), 0), SUB) < slots
    sent = jnp.where(is_row, chosen, live)
    row_msg[:, :, :width] = sent.reshape(n_p, SUB, width)
    row_all[my_p] = row_msg[my_p]

    pl.semaphore_wait(pair_sem.at[0], 1)
    for peer in peers[1:] + peers[:1]:
        tell(feat_sem.at[0], (my_p, peer))

    row_copies = []
    for d in range(1, n_p):
        owner = lax.rem(my_p + d, n_p)
        copy = pltpu.make_async_remote_copy(
            src_ref=row_msg.at[owner], dst_ref=row_all.at[my_p], send_sem=row_send.at[d - 1],
            recv_sem=row_recv.at[d - 1], device_id=(owner, my_f), device_id_type=MESH)
        copy.start()
        row_copies.append(copy)

    for t in range(tiles):
        cen_copies[t].wait()

    @pl.loop(0, tiles)
    def _(t):
        part = pl.ds(pl.multiple_of(t * tile, tile), tile)
        total = jnp.zeros((tile, LANES), f32)
        for b in range(cen.shape[1] // LANES):
            piece = cen[part, b * LANES:(b + 1) * LANES].astype(f32)
            total += piece * piece
        csq[part, :] = jnp.broadcast_to(0.5 * jnp.sum(total, axis=1, keepdims=True), (tile, LANES))

    for copy in part_copies:
        copy.wait()
    label_row = part_msg[...]
    for r in range(n_f - 1):
        label_row = label_row + part_all[r]
    lab_msg[...] = label_row
    lab_all[my_p] = label_row
    lab_copies = []
    for d in range(1, n_p):
        copy = pltpu.make_async_remote_copy(
            src_ref=lab_msg, dst_ref=lab_all.at[my_p], send_sem=lab_send.at[d - 1],
            recv_sem=lab_recv.at[d - 1], device_id=(lax.rem(my_p + d, n_p), my_f), device_id_type=MESH)
        copy.start()
        lab_copies.append(copy)

    start = jnp.full((SUB, crow), jnp.inf, f32)

    def lower(best, gap):
        return jnp.minimum(best, jnp.min(gap.reshape(-1, SUB, crow), axis=0))

    def squares(part):
        return jnp.concatenate([csq[part, :]] * (crow // LANES), axis=1)

    def norm(piece):
        wide = piece.astype(f32)
        return jnp.sum(wide * wide, axis=0, keepdims=True)

    def finish(best, point_sq):
        return point_sq + 2.0 * jnp.min(best, axis=0, keepdims=True)

    pair = 2 * width
    last = pl.cdiv(width, LANES) * LANES
    here = my_f // 2
    away = 1 - here
    here_k = pl.ds(pl.multiple_of(here * pair, LANES), pair)
    lone_k = pl.ds(pl.multiple_of(away * pair + odd * last, LANES), pair - last)
    last_k = pl.ds(pl.multiple_of(away * pair + (1 - odd) * (pair - last), LANES), last)

    def open_chunk(c):
        for copy in slab_copies[c][:2]:
            copy.wait_recv()
        cols = pl.ds(c * crow, crow)
        first = jnp.concatenate([points_ref[here_k, cols], points_ref[lone_k, cols]], axis=0)

        for t in range(centre_count // STEP):
            part = pl.ds(t * STEP, STEP)
            mine = jnp.concatenate([cen[part, here_k], cen[part, lone_k]], axis=1)
            cross = jnp.dot(mine, first, preferred_element_type=f32)
            gap_ref[part, :] = squares(part) - cross

        return norm(first)

    def close_chunk(c, first_sq):
        slab_copies[c][2].wait_recv()
        final = points_ref[last_k, pl.ds(c * crow, crow)]
        point_sq = first_sq + norm(final)

        best = start
        for t in range(centre_count // STEP):
            part = pl.ds(t * STEP, STEP)
            cross = jnp.dot(cen[part, last_k], final, preferred_element_type=f32)
            best = lower(best, gap_ref[part, :] - cross)
        return finish(best, point_sq)

    near_parts = [close_chunk(c, open_chunk(c)) for c in range(chunks - 1)]

    for copy in lab_copies:
        copy.wait()
    for p in range(n_p):
        wide_lab[p * slots:(p + 1) * slots, :] = jnp.broadcast_to(lab_all[p], (slots, LANES))
    wide = wide_lab[...]
    lane_s = lax.broadcasted_iota(jnp.int32, (span, LANES), 1)
    sub_s = lax.broadcasted_iota(jnp.int32, (span, LANES), 0)
    lane_w = lax.broadcasted_iota(jnp.int32, (span, rows_dev), 1) + my_f * rows_dev
    sub_w = lax.broadcasted_iota(jnp.int32, (span, 1), 0)
    for o in range(n_p):
        want = jnp.sum(jnp.where(lane_s == o * slots + lax.rem(sub_s, slots), wide, 0.0),
                       axis=1, keepdims=True) - 1.0
        pick = jnp.full((span, 1), -1, jnp.int32)
        for s in range(slots):
            pick = jnp.where(sub_w == my_p * slots + s, rows_ref[0, s, o], pick)
        hot[o * LANES:o * LANES + span] = jnp.where(want == members, 1.0, 0.0).astype(bf16)
        hot[o * LANES + span:o * LANES + 2 * span] = jnp.where(pick == lane_w, 1.0, 0.0).astype(bf16)
        hot[o * LANES + 2 * span:(o + 1) * LANES] = jnp.zeros((LANES - 2 * span, rows_dev), bf16)

    def summed(values, cols):
        high = values.astype(bf16).astype(f32)
        rest = values - high
        middle = rest.astype(bf16).astype(f32)
        terms = jnp.concatenate([high, middle, rest - middle] + [jnp.ones_like(high)] * 5, axis=0)
        return lax.dot_general(terms.astype(bf16), hot[:, cols], NT, preferred_element_type=f32)

    early = jnp.concatenate(near_parts, axis=1)
    done = summed(early, pl.ds(0, early.shape[1]))
    lane_n = lax.broadcasted_iota(jnp.int32, (1, n_p * LANES), 1)
    later = summed(jnp.zeros((1, crow), f32), pl.ds((chunks - 1) * crow, crow))
    sizes = done[3:4] + later[3:4]
    is_cost = lax.rem(lane_n, LANES) < span
    begun = done[0:1] + done[1:2] + done[2:3] + pltpu.roll(jnp.where(is_cost, sizes, 0.0), 2 * span, 1)

    for copy in row_copies:
        copy.wait()
    sub = lax.broadcasted_iota(jnp.int32, (out_ref.shape[0], LANES), 0)
    lane = lax.broadcasted_iota(jnp.int32, (out_ref.shape[0], LANES), 1)
    out_iota = lax.broadcasted_iota(jnp.int32, out_ref.shape, 0)
    placed = jnp.zeros(out_ref.shape, f32)
    spread = jnp.zeros((out_ref.shape[0], LANES), f32)
    for p in range(n_p):
        block = row_all[p][:, :width]
        for s in range(slots):
            flag = block[slots + s:slots + s + 1] > 0.5
            at = offset_ref[0, p] + s
            placed = jnp.where((out_iota == at) & flag, block[s:s + 1], placed)
            spread = jnp.where((sub == at) & (lane == p * slots + s) & flag[:, :LANES], 1.0, spread)

    first_sq = open_chunk(chunks - 1)
    pl.semaphore_wait(feat_sem.at[0], n_f - 1)
    nearest = close_chunk(chunks - 1, first_sq)
    tail = summed(nearest, pl.ds((chunks - 1) * crow, crow))
    total = begun + tail[0:1] + tail[1:2] + tail[2:3]
    for o in range(n_p):
        red_msg[o] = total[:, o * LANES:(o + 1) * LANES]
    red_all[0] = red_msg[my_p]
    red_copies = []
    for d in range(1, n):
        to = device(d)
        copy = pltpu.make_async_remote_copy(
            src_ref=red_msg.at[to[0]], dst_ref=red_all.at[d], send_sem=red_send.at[d - 1],
            recv_sem=red_recv.at[0], device_id=to, device_id_type=MESH)
        copy.start()
        red_copies.append(copy)
    for copies in slab_copies:
        for copy in copies:
            copy.wait_send()
    for copy in red_copies:
        copy.wait_send()
    pltpu.make_async_remote_copy(
        src_ref=red_all.at[pl.ds(0, n - 1)], dst_ref=red_all.at[pl.ds(1, n - 1)], send_sem=red_send.at[0],
        recv_sem=red_recv.at[0], device_id=device(1), device_id_type=MESH).wait_recv()
    total = jnp.sum(red_all[...], axis=0)
    near = pltpu.roll(total, LANES - span, 1)
    size = pltpu.roll(total, LANES - 2 * span, 1)
    weight = (2.0 * centre_count / (rows_pts * n_p)) / (near / total + 1.0 / size)
    factor = jnp.sum(jnp.where(spread > 0.5, weight, 0.0), axis=1, keepdims=True)
    out_ref[...] = (placed * factor).astype(bf16)


def fused(n_p, n_f, slab, centres, labels, sample_rows, sample_count, slot_offset):
    rows_pts, width = slab.shape
    rows_dev = rows_pts // n_f
    centre_count, depth = centres.shape
    slots = sample_rows.shape[2]
    chunks = rows_dev // CHUNK
    tiles = centre_count // TILE
    n = n_p * n_f
    wide = pl.cdiv(width, LANES) * LANES
    rows_in = sample_rows.transpose(0, 2, 1)
    labels_in = labels.reshape(1, -1)
    dma, regular = pltpu.SemaphoreType.DMA, pltpu.SemaphoreType.REGULAR
    return pl.pallas_call(
        functools.partial(kernel, n_p, n_f, chunks, TILE),
        out_shape=pltpu.VMEM((n_p * slots, width), jnp.bfloat16),
        in_specs=[pl.BlockSpec(memory_space=pl.ANY)] * 6,
        out_specs=pl.BlockSpec(memory_space=pltpu.VMEM),
        scratch_shapes=[
            pltpu.VMEM((centre_count, depth), jnp.bfloat16),
            pltpu.VMEM((centre_count, LANES), jnp.float32),
            pltpu.VMEM((centre_count, CHUNK), jnp.float32),
            pltpu.VMEM((width, rows_pts), jnp.bfloat16),
            pltpu.VMEM((depth, rows_dev), jnp.bfloat16),
            pltpu.VMEM(labels_in.shape, jnp.int32),
            pltpu.SMEM(rows_in.shape, jnp.int32),
            pltpu.SMEM(sample_count.shape, jnp.int32),
            pltpu.SMEM(slot_offset.shape, jnp.int32),
            pltpu.VMEM((1, LANES), jnp.float32),
            pltpu.VMEM((n_f - 1, 1, LANES), jnp.float32),
            pltpu.VMEM((1, LANES), jnp.float32),
            pltpu.VMEM((n_p, 1, LANES), jnp.float32),
            pltpu.VMEM((n_p * slots, LANES), jnp.float32),
            pltpu.VMEM((n_p * LANES, rows_dev), jnp.bfloat16),
            pltpu.VMEM((n_p, SUB, wide), jnp.float32),
            pltpu.VMEM((n_p, SUB, wide), jnp.float32),
            pltpu.VMEM((n_p, 1, LANES), jnp.float32),
            pltpu.VMEM((n, 1, LANES), jnp.float32),
            dma((6,)), dma((tiles,)),
            dma((chunks, n_f - 1)), dma((chunks, n_f - 1)),
            dma((n_f - 1,)), dma((n_f - 1,)),
            dma((n_p - 1,)), dma((n_p - 1,)),
            dma((n_p - 1,)), dma((n_p - 1,)),
            dma((n - 1,)), dma((1,)),
            regular((max(n_p // 2 - 2, 1),)), regular((1,)), regular((1,)),
        ],
        compiler_params=pltpu.CompilerParams(collective_id=0, has_side_effects=True),
    )(slab.T, labels_in, rows_in, sample_count, slot_offset, centres)


def solution(mesh):
    n_p, n_f = mesh.shape["pts"], mesh.shape["feat"]

    def body(slab, centres, labels, sample_rows, sample_count, slot_offset):
        rows_dev = slab.shape[0] // n_f
        slots = sample_rows.shape[2]
        fits = (
            slab.shape[1] % 16 == 0 and rows_dev % CHUNK == 0 and centres.shape[0] % TILE == 0 and TILE % STEP == 0
            and n_f == 4 and 2 * slab.shape[1] % LANES == 0 and slab.shape[1] > LANES and rows_dev // CHUNK > 1
            and 3 * n_p * slots <= LANES and 2 * slots <= SUB and n_p % 2 == 0 and n_p > 2 and n_p * slots % 16 == 0
        )
        args = (slab, centres, labels, sample_rows, sample_count, slot_offset)
        return fused(n_p, n_f, *args) if fits else local(*args)

    placed = (
        P("pts", "feat"),
        P(),
        P(("pts", "feat"), None),
        P("pts", None, None),
        P("pts", None),
        P("pts", None),
    )
    return jax.shard_map(
        body, mesh=mesh, in_specs=placed, out_specs=P("pts", "feat"), check_vma=False
    )
```

```python
import functools

import jax
import jax.numpy as jnp
from jax import lax
from jax.experimental import pallas as pl
from jax.experimental.pallas import tpu as pltpu
from jax.sharding import PartitionSpec as P

NT = (((1,), (1,)), ((), ()))
LANES = 128
SUB = 8
CHUNK = 256
TILE = 2048
STEP = 512
MESH = pl.DeviceIdType.MESH


def local(slab, centres, labels, sample_rows, sample_count, slot_offset):
    rows_pts, feat_width = slab.shape
    feat_count = lax.axis_size("feat")
    rows_dev = rows_pts // feat_count
    centre_count = centres.shape[0]
    centre_sq = jnp.sum(jnp.square(centres.astype(jnp.float32)), axis=1)
    stacked = slab.reshape(feat_count, rows_dev, feat_width)
    points = lax.all_to_all(stacked, "feat", split_axis=0, concat_axis=2, tiled=True)[0]
    cross_term = lax.dot_general(points, centres, NT, preferred_element_type=jnp.float32)
    point_sq = jnp.sum(jnp.square(points.astype(jnp.float32)), axis=1)
    nearest = jnp.min(point_sq[:, None] + centre_sq[None, :] - 2.0 * cross_term, axis=1)[None, :][0]
    member = labels[:, 0]
    cost_part = jax.ops.segment_sum(nearest, member, num_segments=centre_count)
    size_part = jax.ops.segment_sum(jnp.ones_like(nearest), member, num_segments=centre_count)
    cluster_cost, cluster_size = lax.psum((cost_part, size_part), ("pts", "feat"))
    own_sens = nearest / jnp.take(cluster_cost, member) + 1.0 / jnp.take(cluster_size, member)
    shard_sens = lax.all_gather(own_sens, "feat", axis=0, tiled=True)
    total_points = rows_pts * lax.axis_size("pts")
    weight = 2.0 * centre_count / total_points / shard_sens
    picked_rows = sample_rows[0]
    owner_count, slot_count = picked_rows.shape
    chosen = jnp.take(slab, picked_rows.reshape(-1), axis=0).reshape(
        owner_count, slot_count, feat_width
    )
    chosen_weight = jnp.take(weight, picked_rows)
    live_slot = jnp.arange(slot_count, dtype=jnp.int32)[None, :] < sample_count[0][:, None]
    scaled = jnp.where(
        live_slot[:, :, None], chosen.astype(jnp.float32) * chosen_weight[:, :, None], 0.0
    ).astype(jnp.bfloat16)
    arrived = lax.all_to_all(scaled, "pts", split_axis=0, concat_axis=0, tiled=True)
    target = slot_offset[0][:, None] + jnp.arange(slot_count, dtype=jnp.int32)[None, :]
    own_rows = arrived.shape[0] * slot_count
    placed = jnp.zeros((own_rows, feat_width), jnp.float32)
    placed = placed.at[target.reshape(-1)].add(
        arrived.reshape(-1, feat_width).astype(jnp.float32), mode="drop"
    )
    return placed.astype(jnp.bfloat16)


def kernel(n_p, n_f, chunks, tile, slab_hbm, labels_hbm, rows_hbm, count_hbm, offset_hbm, cen_hbm,
           out_ref, cen, csq, gap_ref, slab_ref, points_ref, labels_ref, rows_ref, count_ref, offset_ref,
           part_msg, part_all, lab_msg, lab_all, wide_lab, hot, row_msg, row_all, red_msg, red_all,
           in_sem, cen_sem, a_send, a_recv, part_send, part_recv, lab_send, lab_recv, row_send, row_recv,
           red_send, red_recv, hop_sem, pair_sem, feat_sem):
    f32, bf16 = jnp.float32, jnp.bfloat16
    width, rows_pts = slab_ref.shape
    rows_dev = rows_pts // n_f
    crow = rows_dev // chunks
    n = n_p * n_f
    centre_count = cen.shape[0]
    slots = rows_ref.shape[1]
    span = n_p * slots
    tiles = centre_count // tile
    my_p, my_f = lax.axis_index("pts"), lax.axis_index("feat")
    me = my_p * n_f + my_f

    def device(d):
        other = lax.rem(me + d, n)
        return other // n_f, lax.rem(other, n_f)

    def tell(sem, where):
        pl.semaphore_signal(sem, inc=1, device_id=where, device_id_type=MESH)

    def all_of(ref, sends, arrivals):
        return pltpu.make_async_remote_copy(
            src_ref=ref, dst_ref=ref, send_sem=sends.at[0], recv_sem=arrivals.at[0],
            device_id=device(1), device_id_type=MESH)

    odd = lax.rem(my_f, 2)
    partner = my_f + 1 - 2 * odd
    peers = [partner, lax.rem(my_f + 2, n_f), lax.rem(partner + 2, n_f)]
    twin = my_p + 1 - 2 * lax.rem(my_p, 2)
    has_down, has_up = my_p >= 2, my_p < n_p - 2
    links = jnp.where(has_down, 1, 0) + jnp.where(has_up, 1, 0)

    def tell_chain(sem):
        @pl.when(has_down)
        def _():
            tell(sem, (my_p - 2, my_f))

        @pl.when(has_up)
        def _():
            tell(sem, (my_p + 2, my_f))

    barrier = pltpu.get_barrier_semaphore()
    for peer in peers[1:] + peers[:1]:
        tell(barrier, (my_p, peer))
    tell(barrier, (twin, my_f))
    tell_chain(barrier)

    own_k = pl.ds(pl.multiple_of(my_f * width, width), width)
    own_cols = pl.ds(pl.multiple_of(my_f * rows_dev, rows_dev), rows_dev)
    in_copies = [
        pltpu.make_async_copy(rows_hbm, rows_ref, in_sem.at[0]),
        pltpu.make_async_copy(labels_hbm, labels_ref, in_sem.at[1]),
        pltpu.make_async_copy(count_hbm, count_ref, in_sem.at[2]),
        pltpu.make_async_copy(offset_hbm, offset_ref, in_sem.at[3]),
        pltpu.make_async_copy(slab_hbm, slab_ref, in_sem.at[4]),
        pltpu.make_async_copy(slab_hbm.at[:, own_cols], points_ref.at[own_k], in_sem.at[5]),
    ]
    for copy in in_copies:
        copy.start()
    cen_copy = pltpu.make_async_copy(cen_hbm, cen, cen_sem.at[0])
    cen_copy.start()

    pl.semaphore_wait(barrier, n_f + links)

    slab_copies = []
    for c in range(chunks):
        copies = []
        for r, peer in enumerate(peers):
            at = pl.multiple_of(peer * rows_dev + c * crow, crow)
            copies.append(pltpu.make_async_remote_copy(
                src_ref=slab_hbm.at[:, pl.ds(at, crow)],
                dst_ref=points_ref.at[own_k, pl.ds(c * crow, crow)],
                send_sem=a_send.at[0], recv_sem=a_recv.at[c, r],
                device_id=(my_p, peer), device_id_type=MESH))
        slab_copies.append(copies)
    for c, r in [(0, 1), (0, 0)] + [(c, 0) for c in range(1, chunks)]:
        slab_copies[c][r].start()

    rounds = n_p // 2 - 2
    if rounds:
        tell_chain(hop_sem.at[0])

    for copy in in_copies[:2]:
        copy.wait()
    queries = n_p * SUB
    query_sub = lax.broadcasted_iota(jnp.int32, (queries, 1), 0)
    picked = jnp.full((queries, 1), -1, jnp.int32)
    for o in range(n_p):
        for s in range(slots):
            picked = jnp.where(query_sub == o * SUB + s, rows_ref[0, s, o], picked)
    members = labels_ref[...].astype(f32)
    lane_dev = lax.broadcasted_iota(jnp.int32, (queries, rows_dev), 1)
    own_hit = (lane_dev + my_f * rows_dev) == picked
    own_label = jnp.sum(jnp.where(own_hit, members + 1.0, 0.0), axis=1, keepdims=True)
    lane_q = lax.broadcasted_iota(jnp.int32, (queries, LANES), 1)
    sub_q = lax.broadcasted_iota(jnp.int32, (queries, LANES), 0)
    to_lane = (lax.rem(sub_q, SUB) < slots) & (lane_q == sub_q // SUB * slots + lax.rem(sub_q, SUB))
    part_msg[...] = jnp.sum(jnp.where(to_lane, own_label, 0.0), axis=0, keepdims=True)
    for r, peer in enumerate(peers):
        copy = pltpu.make_async_remote_copy(
            src_ref=part_msg, dst_ref=part_all.at[r], send_sem=part_send.at[0],
            recv_sem=part_recv.at[0], device_id=(my_p, peer), device_id_type=MESH)
        copy.start()
    for c, r in [(0, 2)] + [(c, r) for c in range(1, chunks) for r in (1, 2)]:
        slab_copies[c][r].start()

    for k in range(rounds):
        pl.semaphore_wait(hop_sem.at[k], links)
        if k + 1 < rounds:
            tell_chain(hop_sem.at[k + 1])
    tell(pair_sem.at[0], (twin, my_f))

    for copy in in_copies[2:]:
        copy.wait()
    lane_pts = lax.broadcasted_iota(jnp.int32, (queries, rows_pts), 1)
    chosen = jnp.where(lane_pts == picked, 1.0, 0.0).astype(bf16)
    chosen = lax.dot_general(chosen, slab_ref[...], NT, preferred_element_type=f32)
    live = jnp.zeros((queries, 1), f32)
    for o in range(n_p):
        for s in range(slots):
            flag = jnp.where(count_ref[0, o] > s, 1.0, 0.0)
            live = jnp.where(query_sub == o * SUB + slots + s, flag, live)
    is_row = lax.rem(lax.broadcasted_iota(jnp.int32, (queries, width), 0), SUB) < slots
    sent = jnp.where(is_row, chosen, live)
    row_msg[:, :, :width] = sent.reshape(n_p, SUB, width)
    row_all[my_p] = row_msg[my_p]

    pl.semaphore_wait(pair_sem.at[0], 1)
    for peer in peers[1:] + peers[:1]:
        tell(feat_sem.at[0], (my_p, peer))

    for d in range(1, n_p):
        owner = lax.rem(my_p + d, n_p)
        copy = pltpu.make_async_remote_copy(
            src_ref=row_msg.at[owner], dst_ref=row_all.at[my_p], send_sem=row_send.at[0],
            recv_sem=row_recv.at[0], device_id=(owner, my_f), device_id_type=MESH)
        copy.start()

    cen_copy.wait()

    @pl.loop(0, tiles)
    def _(t):
        part = pl.ds(pl.multiple_of(t * tile, tile), tile)
        total = jnp.zeros((tile, LANES), f32)
        for b in range(cen.shape[1] // LANES):
            piece = cen[part, b * LANES:(b + 1) * LANES].astype(f32)
            total += piece * piece
        csq[part, :] = jnp.broadcast_to(0.5 * jnp.sum(total, axis=1, keepdims=True), (tile, LANES))

    all_of(part_all, part_send, part_recv).wait()
    label_row = part_msg[...]
    for r in range(n_f - 1):
        label_row = label_row + part_all[r]
    lab_msg[...] = label_row
    lab_all[my_p] = label_row
    for d in range(1, n_p):
        copy = pltpu.make_async_remote_copy(
            src_ref=lab_msg, dst_ref=lab_all.at[my_p], send_sem=lab_send.at[0],
            recv_sem=lab_recv.at[0], device_id=(lax.rem(my_p + d, n_p), my_f), device_id_type=MESH)
        copy.start()

    start = jnp.full((SUB, crow), jnp.inf, f32)

    def lower(best, gap):
        return jnp.minimum(best, jnp.min(gap.reshape(-1, SUB, crow), axis=0))

    def squares(part):
        return jnp.concatenate([csq[part, :]] * (crow // LANES), axis=1)

    def norm(piece):
        wide = piece.astype(f32)
        return jnp.sum(wide * wide, axis=0, keepdims=True)

    def finish(best, point_sq):
        return point_sq + 2.0 * jnp.min(best, axis=0, keepdims=True)

    pair = 2 * width
    last = pl.cdiv(width, LANES) * LANES
    here = my_f // 2
    away = 1 - here
    here_k = pl.ds(pl.multiple_of(here * pair, LANES), pair)
    lone_k = pl.ds(pl.multiple_of(away * pair + odd * last, LANES), pair - last)
    last_k = pl.ds(pl.multiple_of(away * pair + (1 - odd) * (pair - last), LANES), last)

    def open_chunk(c):
        for copy in slab_copies[c][:2]:
            copy.wait_recv()
        cols = pl.ds(c * crow, crow)
        first = jnp.concatenate([points_ref[here_k, cols], points_ref[lone_k, cols]], axis=0)

        for t in range(centre_count // STEP):
            part = pl.ds(t * STEP, STEP)
            mine = jnp.concatenate([cen[part, here_k], cen[part, lone_k]], axis=1)
            cross = jnp.dot(mine, first, preferred_element_type=f32)
            gap_ref[part, :] = squares(part) - cross

        return norm(first)

    def close_chunk(c, first_sq):
        slab_copies[c][2].wait_recv()
        final = points_ref[last_k, pl.ds(c * crow, crow)]
        point_sq = first_sq + norm(final)

        best = start
        for t in range(centre_count // STEP):
            part = pl.ds(t * STEP, STEP)
            cross = jnp.dot(cen[part, last_k], final, preferred_element_type=f32)
            best = lower(best, gap_ref[part, :] - cross)
        return finish(best, point_sq)

    near_parts = [close_chunk(c, open_chunk(c)) for c in range(chunks - 1)]

    all_of(lab_all.at[pl.ds(0, n_p - 1)], lab_send, lab_recv).wait()
    for p in range(n_p):
        wide_lab[p * slots:(p + 1) * slots, :] = jnp.broadcast_to(lab_all[p], (slots, LANES))
    wide = wide_lab[...]
    lane_s = lax.broadcasted_iota(jnp.int32, (span, LANES), 1)
    sub_s = lax.broadcasted_iota(jnp.int32, (span, LANES), 0)
    lane_w = lax.broadcasted_iota(jnp.int32, (span, rows_dev), 1) + my_f * rows_dev
    sub_w = lax.broadcasted_iota(jnp.int32, (span, 1), 0)
    for o in range(n_p):
        want = jnp.sum(jnp.where(lane_s == o * slots + lax.rem(sub_s, slots), wide, 0.0),
                       axis=1, keepdims=True) - 1.0
        pick = jnp.full((span, 1), -1, jnp.int32)
        for s in range(slots):
            pick = jnp.where(sub_w == my_p * slots + s, rows_ref[0, s, o], pick)
        hot[o * LANES:o * LANES + span] = jnp.where(want == members, 1.0, 0.0).astype(bf16)
        hot[o * LANES + span:o * LANES + 2 * span] = jnp.where(pick == lane_w, 1.0, 0.0).astype(bf16)
        hot[o * LANES + 2 * span:(o + 1) * LANES] = jnp.zeros((LANES - 2 * span, rows_dev), bf16)

    def summed(values, cols):
        high = values.astype(bf16).astype(f32)
        rest = values - high
        middle = rest.astype(bf16).astype(f32)
        terms = jnp.concatenate([high, middle, rest - middle] + [jnp.ones_like(high)] * 5, axis=0)
        return lax.dot_general(terms.astype(bf16), hot[:, cols], NT, preferred_element_type=f32)

    early = jnp.concatenate(near_parts, axis=1)
    done = summed(early, pl.ds(0, early.shape[1]))
    lane_n = lax.broadcasted_iota(jnp.int32, (1, n_p * LANES), 1)
    later = summed(jnp.zeros((1, crow), f32), pl.ds((chunks - 1) * crow, crow))
    sizes = done[3:4] + later[3:4]
    is_cost = lax.rem(lane_n, LANES) < span
    begun = done[0:1] + done[1:2] + done[2:3] + pltpu.roll(jnp.where(is_cost, sizes, 0.0), 2 * span, 1)

    all_of(row_all.at[pl.ds(0, n_p - 1)], row_send, row_recv).wait()
    sub = lax.broadcasted_iota(jnp.int32, (out_ref.shape[0], LANES), 0)
    lane = lax.broadcasted_iota(jnp.int32, (out_ref.shape[0], LANES), 1)
    out_iota = lax.broadcasted_iota(jnp.int32, out_ref.shape, 0)
    placed = jnp.zeros(out_ref.shape, f32)
    spread = jnp.zeros((out_ref.shape[0], LANES), f32)
    for p in range(n_p):
        block = row_all[p][:, :width]
        for s in range(slots):
            flag = block[slots + s:slots + s + 1] > 0.5
            at = offset_ref[0, p] + s
            placed = jnp.where((out_iota == at) & flag, block[s:s + 1], placed)
            spread = jnp.where((sub == at) & (lane == p * slots + s) & flag[:, :LANES], 1.0, spread)

    first_sq = open_chunk(chunks - 1)
    pl.semaphore_wait(feat_sem.at[0], n_f - 1)
    nearest = close_chunk(chunks - 1, first_sq)
    tail = summed(nearest, pl.ds((chunks - 1) * crow, crow))
    total = begun + tail[0:1] + tail[1:2] + tail[2:3]
    for o in range(n_p):
        red_msg[o] = total[:, o * LANES:(o + 1) * LANES]
    red_all[0] = red_msg[my_p]
    for d in range(1, n):
        to = device(d)
        copy = pltpu.make_async_remote_copy(
            src_ref=red_msg.at[to[0]], dst_ref=red_all.at[d], send_sem=red_send.at[0],
            recv_sem=red_recv.at[0], device_id=to, device_id_type=MESH)
        copy.start()
    all_of(points_ref.at[pl.ds(0, (n_f - 1) * width)], a_send, red_recv).wait_send()
    all_of(red_all.at[pl.ds(0, n - 1)], red_send, red_recv).wait()
    total = jnp.sum(red_all[...], axis=0)
    near = pltpu.roll(total, LANES - span, 1)
    size = pltpu.roll(total, LANES - 2 * span, 1)
    weight = (2.0 * centre_count / (rows_pts * n_p)) / (near / total + 1.0 / size)
    factor = jnp.sum(jnp.where(spread > 0.5, weight, 0.0), axis=1, keepdims=True)
    out_ref[...] = (placed * factor).astype(bf16)


def fused(n_p, n_f, slab, centres, labels, sample_rows, sample_count, slot_offset):
    rows_pts, width = slab.shape
    rows_dev = rows_pts // n_f
    centre_count, depth = centres.shape
    slots = sample_rows.shape[2]
    chunks = rows_dev // CHUNK
    tiles = centre_count // TILE
    n = n_p * n_f
    wide = pl.cdiv(width, LANES) * LANES
    rows_in = sample_rows.transpose(0, 2, 1)
    labels_in = labels.reshape(1, -1)
    dma, regular = pltpu.SemaphoreType.DMA, pltpu.SemaphoreType.REGULAR
    return pl.pallas_call(
        functools.partial(kernel, n_p, n_f, chunks, TILE),
        out_shape=pltpu.VMEM((n_p * slots, width), jnp.bfloat16),
        in_specs=[pl.BlockSpec(memory_space=pl.ANY)] * 6,
        out_specs=pl.BlockSpec(memory_space=pltpu.VMEM),
        scratch_shapes=[
            pltpu.VMEM((centre_count, depth), jnp.bfloat16),
            pltpu.VMEM((centre_count, LANES), jnp.float32),
            pltpu.VMEM((centre_count, CHUNK), jnp.float32),
            pltpu.VMEM((width, rows_pts), jnp.bfloat16),
            pltpu.VMEM((depth, rows_dev), jnp.bfloat16),
            pltpu.VMEM(labels_in.shape, jnp.int32),
            pltpu.SMEM(rows_in.shape, jnp.int32),
            pltpu.SMEM(sample_count.shape, jnp.int32),
            pltpu.SMEM(slot_offset.shape, jnp.int32),
            pltpu.VMEM((1, LANES), jnp.float32),
            pltpu.VMEM((n_f - 1, 1, LANES), jnp.float32),
            pltpu.VMEM((1, LANES), jnp.float32),
            pltpu.VMEM((n_p, 1, LANES), jnp.float32),
            pltpu.VMEM((n_p * slots, LANES), jnp.float32),
            pltpu.VMEM((n_p * LANES, rows_dev), jnp.bfloat16),
            pltpu.VMEM((n_p, SUB, wide), jnp.float32),
            pltpu.VMEM((n_p, SUB, wide), jnp.float32),
            pltpu.VMEM((n_p, 1, LANES), jnp.float32),
            pltpu.VMEM((n, 1, LANES), jnp.float32),
            dma((6,)), dma((1,)),
            dma((1,)), dma((chunks, n_f - 1)),
            dma((1,)), dma((1,)),
            dma((1,)), dma((1,)),
            dma((1,)), dma((1,)),
            dma((1,)), dma((1,)),
            regular((max(n_p // 2 - 2, 1),)), regular((1,)), regular((1,)),
        ],
        compiler_params=pltpu.CompilerParams(collective_id=0, has_side_effects=True),
    )(slab.T, labels_in, rows_in, sample_count, slot_offset, centres)


def solution(mesh):
    n_p, n_f = mesh.shape["pts"], mesh.shape["feat"]

    def body(slab, centres, labels, sample_rows, sample_count, slot_offset):
        rows_dev = slab.shape[0] // n_f
        slots = sample_rows.shape[2]
        fits = (
            slab.shape[1] % 16 == 0 and rows_dev % CHUNK == 0 and centres.shape[0] % TILE == 0 and TILE % STEP == 0
            and n_f == 4 and 2 * slab.shape[1] % LANES == 0 and slab.shape[1] > LANES and rows_dev // CHUNK > 1
            and 3 * n_p * slots <= LANES and 2 * slots <= SUB and n_p % 2 == 0 and n_p > 2 and n_p * slots % 16 == 0
        )
        args = (slab, centres, labels, sample_rows, sample_count, slot_offset)
        return fused(n_p, n_f, *args) if fits else local(*args)

    placed = (
        P("pts", "feat"),
        P(),
        P(("pts", "feat"), None),
        P("pts", None, None),
        P("pts", None),
        P("pts", None),
    )
    return jax.shard_map(
        body, mesh=mesh, in_specs=placed, out_specs=P("pts", "feat"), check_vma=False
    )
```

```python
import functools

import jax
import jax.numpy as jnp
from jax import lax
from jax.experimental import pallas as pl
from jax.experimental.pallas import tpu as pltpu
from jax.sharding import PartitionSpec as P

NT = (((1,), (1,)), ((), ()))
LANES = 128
SUB = 8
CHUNK = 256
TILE = 2048
STEP = 512
MESH = pl.DeviceIdType.MESH


def local(slab, centres, labels, sample_rows, sample_count, slot_offset):
    rows_pts, feat_width = slab.shape
    feat_count = lax.axis_size("feat")
    rows_dev = rows_pts // feat_count
    centre_count = centres.shape[0]
    centre_sq = jnp.sum(jnp.square(centres.astype(jnp.float32)), axis=1)
    stacked = slab.reshape(feat_count, rows_dev, feat_width)
    points = lax.all_to_all(stacked, "feat", split_axis=0, concat_axis=2, tiled=True)[0]
    cross_term = lax.dot_general(points, centres, NT, preferred_element_type=jnp.float32)
    point_sq = jnp.sum(jnp.square(points.astype(jnp.float32)), axis=1)
    nearest = jnp.min(point_sq[:, None] + centre_sq[None, :] - 2.0 * cross_term, axis=1)[None, :][0]
    member = labels[:, 0]
    cost_part = jax.ops.segment_sum(nearest, member, num_segments=centre_count)
    size_part = jax.ops.segment_sum(jnp.ones_like(nearest), member, num_segments=centre_count)
    cluster_cost, cluster_size = lax.psum((cost_part, size_part), ("pts", "feat"))
    own_sens = nearest / jnp.take(cluster_cost, member) + 1.0 / jnp.take(cluster_size, member)
    shard_sens = lax.all_gather(own_sens, "feat", axis=0, tiled=True)
    total_points = rows_pts * lax.axis_size("pts")
    weight = 2.0 * centre_count / total_points / shard_sens
    picked_rows = sample_rows[0]
    owner_count, slot_count = picked_rows.shape
    chosen = jnp.take(slab, picked_rows.reshape(-1), axis=0).reshape(
        owner_count, slot_count, feat_width
    )
    chosen_weight = jnp.take(weight, picked_rows)
    live_slot = jnp.arange(slot_count, dtype=jnp.int32)[None, :] < sample_count[0][:, None]
    scaled = jnp.where(
        live_slot[:, :, None], chosen.astype(jnp.float32) * chosen_weight[:, :, None], 0.0
    ).astype(jnp.bfloat16)
    arrived = lax.all_to_all(scaled, "pts", split_axis=0, concat_axis=0, tiled=True)
    target = slot_offset[0][:, None] + jnp.arange(slot_count, dtype=jnp.int32)[None, :]
    own_rows = arrived.shape[0] * slot_count
    placed = jnp.zeros((own_rows, feat_width), jnp.float32)
    placed = placed.at[target.reshape(-1)].add(
        arrived.reshape(-1, feat_width).astype(jnp.float32), mode="drop"
    )
    return placed.astype(jnp.bfloat16)


def kernel(n_p, n_f, chunks, tile, slab_hbm, labels_hbm, rows_hbm, count_hbm, offset_hbm, cen_hbm,
           out_ref, cen, csq, gap_ref, slab_ref, points_ref, labels_ref, rows_ref, count_ref, offset_ref,
           part_msg, part_all, lab_msg, lab_all, wide_lab, hot, row_msg, row_all, red_msg, red_all,
           in_sem, cen_sem, a_send, a_recv, part_send, part_recv, lab_send, lab_recv, row_send, row_recv,
           red_send, red_recv, hop_sem, pair_sem, feat_sem):
    f32, bf16 = jnp.float32, jnp.bfloat16
    width, rows_pts = slab_ref.shape
    rows_dev = rows_pts // n_f
    crow = rows_dev // chunks
    n = n_p * n_f
    centre_count = cen.shape[0]
    slots = rows_ref.shape[1]
    span = n_p * slots
    tiles = centre_count // tile
    my_p, my_f = lax.axis_index("pts"), lax.axis_index("feat")
    me = my_p * n_f + my_f

    def device(d):
        other = lax.rem(me + d, n)
        return other // n_f, lax.rem(other, n_f)

    def tell(sem, where):
        pl.semaphore_signal(sem, inc=1, device_id=where, device_id_type=MESH)

    def all_of(ref, sends, arrivals):
        return pltpu.make_async_remote_copy(
            src_ref=ref, dst_ref=ref, send_sem=sends.at[0], recv_sem=arrivals.at[0],
            device_id=device(1), device_id_type=MESH)

    odd = lax.rem(my_f, 2)
    partner = my_f + 1 - 2 * odd
    peers = [partner, lax.rem(my_f + 2, n_f), lax.rem(partner + 2, n_f)]
    twin = my_p + 1 - 2 * lax.rem(my_p, 2)
    has_down, has_up = my_p >= 2, my_p < n_p - 2
    links = jnp.where(has_down, 1, 0) + jnp.where(has_up, 1, 0)

    def tell_chain(sem):
        @pl.when(has_down)
        def _():
            tell(sem, (my_p - 2, my_f))

        @pl.when(has_up)
        def _():
            tell(sem, (my_p + 2, my_f))

    barrier = pltpu.get_barrier_semaphore()
    for peer in peers[1:] + peers[:1]:
        tell(barrier, (my_p, peer))
    tell(barrier, (twin, my_f))
    tell_chain(barrier)

    own_k = pl.ds(pl.multiple_of(my_f * width, width), width)
    own_cols = pl.ds(pl.multiple_of(my_f * rows_dev, rows_dev), rows_dev)
    in_copies = [
        pltpu.make_async_copy(rows_hbm, rows_ref, in_sem.at[0]),
        pltpu.make_async_copy(labels_hbm, labels_ref, in_sem.at[1]),
        pltpu.make_async_copy(count_hbm, count_ref, in_sem.at[2]),
        pltpu.make_async_copy(offset_hbm, offset_ref, in_sem.at[3]),
        pltpu.make_async_copy(slab_hbm, slab_ref, in_sem.at[4]),
        pltpu.make_async_copy(slab_hbm.at[:, own_cols], points_ref.at[own_k], in_sem.at[5]),
    ]
    for copy in in_copies:
        copy.start()
    cen_copy = pltpu.make_async_copy(cen_hbm, cen, cen_sem.at[0])
    cen_copy.start()

    pl.semaphore_wait(barrier, n_f + links)

    slab_copies = []
    for c in range(chunks):
        copies = []
        for r, peer in enumerate(peers):
            at = pl.multiple_of(peer * rows_dev + c * crow, crow)
            copies.append(pltpu.make_async_remote_copy(
                src_ref=slab_hbm.at[:, pl.ds(at, crow)],
                dst_ref=points_ref.at[own_k, pl.ds(c * crow, crow)],
                send_sem=a_send.at[0], recv_sem=a_recv.at[c, r],
                device_id=(my_p, peer), device_id_type=MESH))
        slab_copies.append(copies)
    for c, r in [(0, 1), (0, 0)] + [(c, 0) for c in range(1, chunks)]:
        slab_copies[c][r].start()

    rounds = n_p // 2 - 2
    if rounds:
        tell_chain(hop_sem.at[0])

    for copy in in_copies[:2]:
        copy.wait()
    queries = n_p * SUB
    query_sub = lax.broadcasted_iota(jnp.int32, (queries, 1), 0)
    picked = jnp.full((queries, 1), -1, jnp.int32)
    for o in range(n_p):
        for s in range(slots):
            picked = jnp.where(query_sub == o * SUB + s, rows_ref[0, s, o], picked)
    members = labels_ref[...].astype(f32)
    lane_dev = lax.broadcasted_iota(jnp.int32, (queries, rows_dev), 1)
    own_hit = (lane_dev + my_f * rows_dev) == picked
    own_label = jnp.sum(jnp.where(own_hit, members + 1.0, 0.0), axis=1, keepdims=True)
    lane_q = lax.broadcasted_iota(jnp.int32, (queries, LANES), 1)
    sub_q = lax.broadcasted_iota(jnp.int32, (queries, LANES), 0)
    to_lane = (lax.rem(sub_q, SUB) < slots) & (lane_q == sub_q // SUB * slots + lax.rem(sub_q, SUB))
    part_msg[...] = jnp.sum(jnp.where(to_lane, own_label, 0.0), axis=0, keepdims=True)
    for r, peer in enumerate(peers):
        copy = pltpu.make_async_remote_copy(
            src_ref=part_msg, dst_ref=part_all.at[r], send_sem=part_send.at[0],
            recv_sem=part_recv.at[0], device_id=(my_p, peer), device_id_type=MESH)
        copy.start()
    for c, r in [(0, 2)] + [(c, r) for c in range(1, chunks) for r in (1, 2)]:
        slab_copies[c][r].start()

    for k in range(rounds):
        pl.semaphore_wait(hop_sem.at[k], links)
        if k + 1 < rounds:
            tell_chain(hop_sem.at[k + 1])
    tell(pair_sem.at[0], (twin, my_f))

    for copy in in_copies[2:]:
        copy.wait()
    lane_pts = lax.broadcasted_iota(jnp.int32, (queries, rows_pts), 1)
    chosen = jnp.where(lane_pts == picked, 1.0, 0.0).astype(bf16)
    chosen = lax.dot_general(chosen, slab_ref[...], NT, preferred_element_type=f32)
    live = jnp.zeros((queries, 1), f32)
    for o in range(n_p):
        for s in range(slots):
            flag = jnp.where(count_ref[0, o] > s, 1.0, 0.0)
            live = jnp.where(query_sub == o * SUB + slots + s, flag, live)
    is_row = lax.rem(lax.broadcasted_iota(jnp.int32, (queries, width), 0), SUB) < slots
    sent = jnp.where(is_row, chosen, live)
    row_msg[:, :, :width] = sent.reshape(n_p, SUB, width)
    row_all[my_p] = row_msg[my_p]

    pl.semaphore_wait(pair_sem.at[0], 1)
    for peer in peers[1:] + peers[:1]:
        tell(feat_sem.at[0], (my_p, peer))

    for d in range(1, n_p):
        owner = lax.rem(my_p + d, n_p)
        copy = pltpu.make_async_remote_copy(
            src_ref=row_msg.at[owner], dst_ref=row_all.at[my_p], send_sem=row_send.at[0],
            recv_sem=row_recv.at[0], device_id=(owner, my_f), device_id_type=MESH)
        copy.start()

    cen_copy.wait()

    @pl.loop(0, tiles)
    def _(t):
        part = pl.ds(pl.multiple_of(t * tile, tile), tile)
        total = jnp.zeros((tile, LANES), f32)
        for b in range(cen.shape[1] // LANES):
            piece = cen[part, b * LANES:(b + 1) * LANES].astype(f32)
            total += piece * piece
        csq[part, :] = jnp.broadcast_to(0.5 * jnp.sum(total, axis=1, keepdims=True), (tile, LANES))

    all_of(part_all, part_send, part_recv).wait()
    label_row = part_msg[...]
    for r in range(n_f - 1):
        label_row = label_row + part_all[r]
    lab_msg[...] = label_row
    lab_all[my_p] = label_row
    for d in range(1, n_p):
        copy = pltpu.make_async_remote_copy(
            src_ref=lab_msg, dst_ref=lab_all.at[my_p], send_sem=lab_send.at[0],
            recv_sem=lab_recv.at[0], device_id=(lax.rem(my_p + d, n_p), my_f), device_id_type=MESH)
        copy.start()

    start = jnp.full((SUB, crow), jnp.inf, f32)

    def lower(best, gap):
        return jnp.minimum(best, jnp.min(gap.reshape(-1, SUB, crow), axis=0))

    def squares(part):
        return jnp.concatenate([csq[part, :]] * (crow // LANES), axis=1)

    def norm(piece):
        wide = piece.astype(f32)
        return jnp.sum(wide * wide, axis=0, keepdims=True)

    def finish(best, point_sq):
        return point_sq + 2.0 * jnp.min(best, axis=0, keepdims=True)

    pair = 2 * width
    last = pl.cdiv(width, LANES) * LANES
    here = my_f // 2
    away = 1 - here
    here_k = pl.ds(pl.multiple_of(here * pair, LANES), pair)
    lone_k = pl.ds(pl.multiple_of(away * pair + odd * last, LANES), pair - last)
    last_k = pl.ds(pl.multiple_of(away * pair + (1 - odd) * (pair - last), LANES), last)

    def open_chunk(c):
        for copy in slab_copies[c][:2]:
            copy.wait_recv()
        cols = pl.ds(c * crow, crow)
        first = jnp.concatenate([points_ref[here_k, cols], points_ref[lone_k, cols]], axis=0)

        for t in range(centre_count // STEP):
            part = pl.ds(t * STEP, STEP)
            mine = jnp.concatenate([cen[part, here_k], cen[part, lone_k]], axis=1)
            cross = jnp.dot(mine, first, preferred_element_type=f32)
            gap_ref[part, :] = squares(part) - cross

        return norm(first)

    def close_chunk(c, first_sq):
        slab_copies[c][2].wait_recv()
        final = points_ref[last_k, pl.ds(c * crow, crow)]
        point_sq = first_sq + norm(final)

        best = start
        for t in range(centre_count // STEP):
            part = pl.ds(t * STEP, STEP)
            cross = jnp.dot(cen[part, last_k], final, preferred_element_type=f32)
            best = lower(best, gap_ref[part, :] - cross)
        return finish(best, point_sq)

    lane_w = lax.broadcasted_iota(jnp.int32, (span, rows_dev), 1) + my_f * rows_dev
    sub_w = lax.broadcasted_iota(jnp.int32, (span, 1), 0)
    for o in range(n_p):
        pick = jnp.full((span, 1), -1, jnp.int32)
        for s in range(slots):
            pick = jnp.where(sub_w == my_p * slots + s, rows_ref[0, s, o], pick)
        hot[o * LANES + span:o * LANES + 2 * span] = jnp.where(pick == lane_w, 1.0, 0.0).astype(bf16)
        hot[o * LANES + 2 * span:(o + 1) * LANES] = jnp.zeros((LANES - 2 * span, rows_dev), bf16)

    near_parts = [close_chunk(c, open_chunk(c)) for c in range(chunks - 1)]

    all_of(lab_all.at[pl.ds(0, n_p - 1)], lab_send, lab_recv).wait()
    for p in range(n_p):
        wide_lab[p * slots:(p + 1) * slots, :] = jnp.broadcast_to(lab_all[p], (slots, LANES))
    wide = wide_lab[...]
    lane_s = lax.broadcasted_iota(jnp.int32, (span, LANES), 1)
    sub_s = lax.broadcasted_iota(jnp.int32, (span, LANES), 0)
    for o in range(n_p):
        want = jnp.sum(jnp.where(lane_s == o * slots + lax.rem(sub_s, slots), wide, 0.0),
                       axis=1, keepdims=True) - 1.0
        hot[o * LANES:o * LANES + span] = jnp.where(want == members, 1.0, 0.0).astype(bf16)

    def summed(values, cols):
        high = values.astype(bf16).astype(f32)
        rest = values - high
        middle = rest.astype(bf16).astype(f32)
        terms = jnp.concatenate([high, middle, rest - middle] + [jnp.ones_like(high)] * 5, axis=0)
        return lax.dot_general(terms.astype(bf16), hot[:, cols], NT, preferred_element_type=f32)

    early = jnp.concatenate(near_parts + [jnp.zeros((1, crow), f32)], axis=1)
    done = summed(early, pl.ds(0, rows_dev))
    lane_n = lax.broadcasted_iota(jnp.int32, (1, n_p * LANES), 1)
    is_cost = lax.rem(lane_n, LANES) < span
    begun = done[0:1] + done[1:2] + done[2:3] + pltpu.roll(jnp.where(is_cost, done[3:4], 0.0), 2 * span, 1)

    first_sq = open_chunk(chunks - 1)
    pl.semaphore_wait(feat_sem.at[0], n_f - 1)
    nearest = close_chunk(chunks - 1, first_sq)
    tail = summed(nearest, pl.ds((chunks - 1) * crow, crow))
    total = begun + tail[0:1] + tail[1:2] + tail[2:3]
    for o in range(n_p):
        red_msg[o] = total[:, o * LANES:(o + 1) * LANES]
    red_all[0] = red_msg[my_p]
    for d in range(1, n):
        to = device(d)
        copy = pltpu.make_async_remote_copy(
            src_ref=red_msg.at[to[0]], dst_ref=red_all.at[d], send_sem=red_send.at[0],
            recv_sem=red_recv.at[0], device_id=to, device_id_type=MESH)
        copy.start()
    all_of(row_all.at[pl.ds(0, n_p - 1)], row_send, row_recv).wait()
    sub = lax.broadcasted_iota(jnp.int32, (out_ref.shape[0], LANES), 0)
    lane = lax.broadcasted_iota(jnp.int32, (out_ref.shape[0], LANES), 1)
    out_iota = lax.broadcasted_iota(jnp.int32, out_ref.shape, 0)
    placed = jnp.zeros(out_ref.shape, f32)
    spread = jnp.zeros((out_ref.shape[0], LANES), f32)
    for p in range(n_p):
        block = row_all[p][:, :width]
        for s in range(slots):
            flag = block[slots + s:slots + s + 1] > 0.5
            at = offset_ref[0, p] + s
            placed = jnp.where((out_iota == at) & flag, block[s:s + 1], placed)
            spread = jnp.where((sub == at) & (lane == p * slots + s) & flag[:, :LANES], 1.0, spread)

    all_of(points_ref.at[pl.ds(0, (n_f - 1) * width)], a_send, red_recv).wait_send()
    all_of(red_all.at[pl.ds(0, n - 1)], red_send, red_recv).wait()
    total = jnp.sum(red_all[...], axis=0)
    near = pltpu.roll(total, LANES - span, 1)
    size = pltpu.roll(total, LANES - 2 * span, 1)
    weight = (2.0 * centre_count / (rows_pts * n_p)) / (near / total + 1.0 / size)
    factor = jnp.sum(jnp.where(spread > 0.5, weight, 0.0), axis=1, keepdims=True)
    out_ref[...] = (placed * factor).astype(bf16)


def fused(n_p, n_f, slab, centres, labels, sample_rows, sample_count, slot_offset):
    rows_pts, width = slab.shape
    rows_dev = rows_pts // n_f
    centre_count, depth = centres.shape
    slots = sample_rows.shape[2]
    chunks = rows_dev // CHUNK
    tiles = centre_count // TILE
    n = n_p * n_f
    wide = pl.cdiv(width, LANES) * LANES
    rows_in = sample_rows.transpose(0, 2, 1)
    labels_in = labels.reshape(1, -1)
    dma, regular = pltpu.SemaphoreType.DMA, pltpu.SemaphoreType.REGULAR
    return pl.pallas_call(
        functools.partial(kernel, n_p, n_f, chunks, TILE),
        out_shape=pltpu.VMEM((n_p * slots, width), jnp.bfloat16),
        in_specs=[pl.BlockSpec(memory_space=pl.ANY)] * 6,
        out_specs=pl.BlockSpec(memory_space=pltpu.VMEM),
        scratch_shapes=[
            pltpu.VMEM((centre_count, depth), jnp.bfloat16),
            pltpu.VMEM((centre_count, LANES), jnp.float32),
            pltpu.VMEM((centre_count, CHUNK), jnp.float32),
            pltpu.VMEM((width, rows_pts), jnp.bfloat16),
            pltpu.VMEM((depth, rows_dev), jnp.bfloat16),
            pltpu.VMEM(labels_in.shape, jnp.int32),
            pltpu.SMEM(rows_in.shape, jnp.int32),
            pltpu.SMEM(sample_count.shape, jnp.int32),
            pltpu.SMEM(slot_offset.shape, jnp.int32),
            pltpu.VMEM((1, LANES), jnp.float32),
            pltpu.VMEM((n_f - 1, 1, LANES), jnp.float32),
            pltpu.VMEM((1, LANES), jnp.float32),
            pltpu.VMEM((n_p, 1, LANES), jnp.float32),
            pltpu.VMEM((n_p * slots, LANES), jnp.float32),
            pltpu.VMEM((n_p * LANES, rows_dev), jnp.bfloat16),
            pltpu.VMEM((n_p, SUB, wide), jnp.float32),
            pltpu.VMEM((n_p, SUB, wide), jnp.float32),
            pltpu.VMEM((n_p, 1, LANES), jnp.float32),
            pltpu.VMEM((n, 1, LANES), jnp.float32),
            dma((6,)), dma((1,)),
            dma((1,)), dma((chunks, n_f - 1)),
            dma((1,)), dma((1,)),
            dma((1,)), dma((1,)),
            dma((1,)), dma((1,)),
            dma((1,)), dma((1,)),
            regular((max(n_p // 2 - 2, 1),)), regular((1,)), regular((1,)),
        ],
        compiler_params=pltpu.CompilerParams(collective_id=0, has_side_effects=True),
    )(slab.T, labels_in, rows_in, sample_count, slot_offset, centres)


def solution(mesh):
    n_p, n_f = mesh.shape["pts"], mesh.shape["feat"]

    def body(slab, centres, labels, sample_rows, sample_count, slot_offset):
        rows_dev = slab.shape[0] // n_f
        slots = sample_rows.shape[2]
        fits = (
            slab.shape[1] % 16 == 0 and rows_dev % CHUNK == 0 and centres.shape[0] % TILE == 0 and TILE % STEP == 0
            and n_f == 4 and 2 * slab.shape[1] % LANES == 0 and slab.shape[1] > LANES and rows_dev // CHUNK > 1
            and 3 * n_p * slots <= LANES and 2 * slots <= SUB and n_p % 2 == 0 and n_p > 2 and n_p * slots % 16 == 0
        )
        args = (slab, centres, labels, sample_rows, sample_count, slot_offset)
        return fused(n_p, n_f, *args) if fits else local(*args)

    placed = (
        P("pts", "feat"),
        P(),
        P(("pts", "feat"), None),
        P("pts", None, None),
        P("pts", None),
        P("pts", None),
    )
    return jax.shard_map(
        body, mesh=mesh, in_specs=placed, out_specs=P("pts", "feat"), check_vma=False
    )
```
